128 devices in a mesh: scan: 4 (over y), slab: 32 (over x, z, core).
Axes of the slice: x: 4, y: 4, z: 4, core: 2. Of those that a mesh axis runs over, the one named last changes fastest.
Arguments:
- solution: float32 [6144, 2048], P(('scan', 'slab')), parts along dimension 0, may hold values from -6 to 6
- direction: float32 [6144, 2048], P(('scan', 'slab')), parts along dimension 0, may hold values from -20 to 20
- gradient: float32 [6144, 2048], P(('scan', 'slab')), parts along dimension 0, may hold values from -40 to 40
- residual: float32 [2048, 64, 896], P(('scan', 'slab')), parts along dimension 0, may hold values from -20 to 20
- tiles: bfloat16 [4, 2048, 896], replicated, may hold values from -0.125 to 0.125
- offsets: int32 [2048], P(('scan', 'slab')), parts along dimension 0, may hold values from 1 to 1472, as said below
Outputs:
- solution_next: float32 [6144, 2048], P(('scan', 'slab')), parts along dimension 0
- residual_next: float32 [2048, 64, 896], P(('scan', 'slab')), parts along dimension 0
- gradient_next: float32 [6144, 2048], P(('scan', 'slab')), parts along dimension 0
- direction_next: float32 [6144, 2048], P(('scan', 'slab')), parts along dimension 0
The draws below stay inside these ranges and needn't reach their ends.
There are 4 independent parts, one for each index of `scan`. The reference program is written for one: setup_inputs(seed, part) draws one part's arguments, and reference() takes and returns one part's arrays. A program takes and returns all parts, laid end to end along the dimension named above; an argument that names none is the same for every part. Nothing has to cross between parts.
Inputs may be any that keep to these rules, and one draw needn't show every extreme that they name: View v belongs to slab v // 16, whose planes are s * 48 to s * 48 + 47 for slab s; its window offsets[v] to offsets[v] + 63 meets that slab and lies within the slab before it, the slab itself and the slab after it; offsets are 1 or more.
All inputs are finite; a program needn't handle non-finite values.
Results may differ from the reference program's by a relative error of at most 0.0029.
Values may be sent and summed in bfloat16 or wider, within the bound.
No kernel may reach another device: no remote copies, remote signals or barrier semaphores. Data moves between devices by JAX's collectives and lax.ppermute only.
A program may use at most 192 MiB of HBM per device.

```python
import math
import jax
import jax.numpy as jnp
from jax import lax

ZD = 48
DR = 64
DC = 896
P_SIZE = 2048
VIEW_DEV = 16
ANGLES = 4
NZ = 1536
VIEWS = 512


def rising_draw(key, length, inner_dims):
    positions = jnp.arange(length, dtype=jnp.float32) / max(length - 1, 1)
    rising_scale = jnp.exp(positions * math.log(3.0)).reshape((length,) + (1,) * len(inner_dims))
    values = jnp.clip(jax.random.normal(key, (length,) + inner_dims, jnp.float32), -4.0, 4.0)
    return values * rising_scale


def draw_direction(key, part):
    return rising_draw(jax.random.fold_in(key, 11), NZ, (P_SIZE,))


def draw_gradient(key, part):
    overall = jnp.exp(jax.random.uniform(jax.random.fold_in(key, 21), (), jnp.float32, math.log(0.5), math.log(2.0)))
    return rising_draw(jax.random.fold_in(key, 12), NZ, (P_SIZE,)) * overall


def draw_residual(key, part):
    return rising_draw(jax.random.fold_in(key, 13), VIEWS, (DR, DC))


def draw_offsets(key, part):
    owners = jnp.arange(VIEWS, dtype=jnp.int32) // VIEW_DEV
    lowest = jnp.maximum(jnp.maximum((owners - 1) * ZD, owners * ZD - DR + 1), 1)
    highest = jnp.minimum(jnp.minimum(owners * ZD + ZD - 1, (owners + 2) * ZD - DR), NZ - DR)
    return jax.random.randint(jax.random.fold_in(key, 14), (VIEWS,), lowest, highest + 1, jnp.int32)


def block_levels(rng, extent, cuts, smallest, high):
    gain, own = 1.0, jax.random.fold_in(rng, 6)
    for dim, shards_of in cuts:
        steps = jnp.exp(jax.random.uniform(jax.random.fold_in(own, dim), (shards_of,), jnp.float32, smallest / len(cuts), high / len(cuts)))
        gain = gain * jnp.repeat(steps, extent[dim] // shards_of).reshape([-1 if axis == dim else 1 for axis in range(len(extent))])
    return gain


def scatter_about(own_key, dims, width, most, shards=(), held_as=jnp.bfloat16):
    drawn = width * jax.random.normal(own_key, dims, jnp.float32)
    if shards:
        drawn = drawn * block_levels(own_key, dims, shards, -0.22, 0.18)
    return jnp.clip(drawn, -most, most).astype(held_as)


def setup_inputs(seed: int = 0, part: int = 0) -> dict:
    arg_keys = jax.random.split(jax.random.key(seed), 7)
    part_keys = jax.random.split(jax.random.fold_in(arg_keys[6], part), 7)
    solution = scatter_about(part_keys[0], (NZ, P_SIZE), 1.0, 6.0, ((0, 32),), jnp.float32)
    direction = draw_direction(jax.random.fold_in(jax.random.fold_in(arg_keys[6], part), 71), part)
    gradient = draw_gradient(jax.random.fold_in(jax.random.fold_in(arg_keys[6], part), 71), part)
    residual = draw_residual(jax.random.fold_in(jax.random.fold_in(arg_keys[6], part), 71), part)
    tiles = scatter_about(arg_keys[4], (ANGLES, P_SIZE, DC), P_SIZE ** -0.5, 0.125)
    offsets = draw_offsets(jax.random.fold_in(jax.random.fold_in(arg_keys[6], part), 71), part)
    return dict(solution=solution, direction=direction, gradient=gradient, residual=residual, tiles=tiles, offsets=offsets)


def reference(solution, direction, gradient, residual, tiles, offsets):
    direction_half = direction.astype(jnp.bfloat16)
    view_total = offsets.shape[0]
    angle_ids = (jnp.arange(view_total, dtype=jnp.int32) % ANGLES).astype(jnp.int32)

    def forward_view(carried, view_item):
        first_row, angle_index = view_item
        window_rows = lax.dynamic_slice_in_dim(direction_half, first_row.astype(jnp.int32), DR, 0)
        angle_tile = lax.dynamic_index_in_dim(tiles, angle_index, 0, keepdims=False)
        return carried, jnp.dot(window_rows, angle_tile, preferred_element_type=jnp.float32)

    _, projected = lax.scan(forward_view, jnp.float32(0.0), (offsets, angle_ids))
    grad_norm = jnp.sum(gradient * gradient)
    image_norm = jnp.sum(projected * projected)
    step_size = grad_norm / image_norm
    solution_next = solution + step_size * direction
    residual_next = residual - step_size * projected
    residual_half = residual_next.astype(jnp.bfloat16)

    def backward_view(accumulated, view_item):
        first_row, angle_index, residual_rows = view_item
        angle_tile = lax.dynamic_index_in_dim(tiles, angle_index, 0, keepdims=False)
        contribution = lax.dot_general(residual_rows, angle_tile, (((1,), (1,)), ((), ())), preferred_element_type=jnp.float32)
        first_row = first_row.astype(jnp.int32)
        current = lax.dynamic_slice_in_dim(accumulated, first_row, DR, 0)
        return lax.dynamic_update_slice_in_dim(accumulated, current + contribution, first_row, 0), None

    empty = jnp.zeros((NZ, P_SIZE), jnp.float32)
    gradient_next, _ = lax.scan(backward_view, empty, (offsets, angle_ids, residual_half))
    new_norm = jnp.sum(gradient_next * gradient_next)
    direction_next = gradient_next + (new_norm / grad_norm) * direction
    return solution_next, residual_next, gradient_next, direction_next
```

```python
import jax
import jax.numpy as jnp
from jax import lax
from jax.experimental import pallas as pl
from jax.experimental.pallas import tpu as pltpu
from jax.sharding import PartitionSpec as P

ANGLES = 4
LANES = 128
F32 = jnp.float32
BF16 = jnp.bfloat16
MIB = 1 << 20


def first_plane(offsets, v, slab_rows):
    return offsets[v] - lax.axis_index("slab") * slab_rows + slab_rows


def pair_is_above():
    return lax.rem(lax.axis_index("slab"), 2) == 0


def split(x):
    high = x.astype(BF16)
    return high, (x - high.astype(F32)).astype(BF16)


def lane_sums(x):
    total = x[:, :LANES]
    for j in range(1, x.shape[1] // LANES):
        total = total + x[:, j * LANES : (j + 1) * LANES]
    return jnp.sum(total, axis=0, keepdims=True)


def backproject_residual(offsets, residual_hbm, tiles_hbm, tiles, own, to_pair, to_cross,
                         residual, rows, acc, residual_sem, tiles_sem):
    views, detector_rows, columns = residual.shape
    slab_rows, cells = own.shape[0], tiles.shape[1]
    near = 3 * slab_rows
    blocks = columns // LANES
    parts = 2
    part_cells = cells // parts

    def residual_copy(v):
        return pltpu.make_async_copy(residual_hbm.at[v], residual.at[v], residual_sem.at[v])

    def tile_copy(a, h):
        cut = pl.ds(h * part_cells, part_cells)
        return pltpu.make_async_copy(
            tiles_hbm.at[a, cut], tiles.at[a, cut], tiles_sem.at[a * parts + h]
        )

    order = [g * ANGLES + a for a in range(ANGLES) for g in range(views // ANGLES)]
    for v in order:
        residual_copy(v).start()
    for a in range(ANGLES):
        for h in range(parts):
            tile_copy(a, h).start()

    rows[...] = jnp.zeros_like(rows)
    plane = lax.broadcasted_iota(jnp.int32, (near, LANES), 0)
    lane = lax.broadcasted_iota(jnp.int32, (near, LANES), 1)
    counts = jnp.zeros((near, LANES), F32)
    for v in range(views):
        first = first_plane(offsets, v, slab_rows)
        seen = (plane >= first) & (plane < first + detector_rows) & (lane == v % ANGLES)
        counts = counts + seen.astype(F32)
    acc[:, cells:] = counts

    for a in range(ANGLES):
        for g in range(views // ANGLES):
            v = g * ANGLES + a
            first = first_plane(offsets, v, slab_rows)
            residual_copy(v).wait()
            for j in range(blocks):
                rows[j, pl.ds(first, detector_rows), :] += residual[
                    v, :, j * LANES : (j + 1) * LANES
                ]
        summed = jnp.concatenate([rows[j] for j in range(blocks)], axis=1)
        if a + 1 < ANGLES:
            rows[...] = jnp.zeros_like(rows)
        both = jnp.concatenate(split(summed), axis=0)
        for h in range(parts):
            tile_copy(a, h).wait()
            for b in range(h * part_cells, (h + 1) * part_cells, 512):
                part = lax.dot_general(
                    both, tiles[a, b : b + 512, :], (((1,), (1,)), ((), ())),
                    preferred_element_type=F32,
                )
                part = part[:near] + part[near:]
                if a == 0:
                    acc[:, b : b + 512] = part
                else:
                    acc[:, b : b + 512] += part

    own[...] = acc[slab_rows : 2 * slab_rows, :]
    above = pair_is_above()
    pair_row = pl.multiple_of(jnp.where(above, 2 * slab_rows, 0), 16)
    cross_row = pl.multiple_of(jnp.where(above, 0, 2 * slab_rows), 16)
    to_pair[...] = acc[pl.ds(pair_row, slab_rows), :].astype(BF16)
    to_cross[...] = acc[pl.ds(cross_row, slab_rows), :].astype(BF16)


def project_planes(direction, from_pair, from_cross, gradient, tiles, planes, back, squares,
                   grad_sums, near):
    slab_rows = direction.shape[0]
    columns = tiles.shape[2]
    above = pair_is_above()
    pair_row = pl.multiple_of(jnp.where(above, 2 * slab_rows, 0), 16)
    cross_row = pl.multiple_of(jnp.where(above, 0, 2 * slab_rows), 16)
    near[pl.ds(slab_rows, slab_rows), :] = direction[...].astype(BF16)
    near[pl.ds(pair_row, slab_rows), :] = from_pair[...].astype(BF16)
    near[pl.ds(cross_row, slab_rows), :] = from_cross[...].astype(BF16)
    grad_sums[...] = lane_sums(gradient[...] * gradient[...])
    for a in range(ANGLES):
        image = jnp.dot(near[...], tiles[a], preferred_element_type=F32)
        total = None
        for j in range(columns // LANES):
            block = image[:, j * LANES : (j + 1) * LANES]
            planes[a, j] = block
            mine = block[slab_rows : 2 * slab_rows]
            total = mine * mine if total is None else total + mine * mine
        squares[a] = total
        both = jnp.concatenate(split(image[slab_rows : 2 * slab_rows]), axis=0)
        for b in range(0, tiles.shape[1], 512):
            part = lax.dot_general(
                both, tiles[a, b : b + 512, :], (((1,), (1,)), ((), ())),
                preferred_element_type=F32,
            )
            back[a, :, b : b + 512] = part[:slab_rows] + part[slab_rows:]


def combine(own, from_pair, from_cross, back, squares, grad_sums, residual_part, image_part, sums):
    cells = residual_part.shape[1]
    counts = own[:, cells:] + from_pair[:, cells:].astype(F32) + from_cross[:, cells:].astype(F32)
    zero = jnp.zeros((1, LANES), F32)
    rr, ri, ii = zero, zero, zero
    weights = [counts[:, a : a + 1] for a in range(ANGLES)]
    for b in range(0, cells, 512):
        cut = slice(b, b + 512)
        r = own[:, cut] + from_pair[:, cut].astype(F32) + from_cross[:, cut].astype(F32)
        i = weights[0] * back[0, :, cut]
        for a in range(1, ANGLES):
            i = i + weights[a] * back[a, :, cut]
        residual_part[:, cut] = r
        image_part[:, cut] = i
        rr, ri, ii = rr + lane_sums(r * r), ri + lane_sums(r * i), ii + lane_sums(i * i)
    image_norm = weights[0] * squares[0]
    for a in range(1, ANGLES):
        image_norm = image_norm + weights[a] * squares[a]
    sums[...] = jnp.concatenate(
        [grad_sums[...], lane_sums(image_norm), rr, ri, ii, zero, zero, zero], axis=0
    )


def finish(offsets, sums, solution, direction, residual_part, image_part, planes, residual,
           solution_next, residual_hbm, gradient_next, direction_next, updated, sem):
    views, detector_rows, columns = residual.shape
    slab_rows = solution.shape[0]
    total = jnp.sum(sums[...], axis=1, keepdims=True)
    grad_norm, image_norm = total[0:1], total[1:2]
    step = grad_norm / image_norm
    new_norm = total[2:3] - 2.0 * step * total[3:4] + step * step * total[4:5]
    beta = new_norm / grad_norm

    def out_copy(v):
        return pltpu.make_async_copy(updated.at[v], residual_hbm.at[v], sem.at[v])

    for v in range(views):
        first = first_plane(offsets, v, slab_rows)
        for j in range(columns // LANES):
            cut = slice(j * LANES, (j + 1) * LANES)
            updated[v, :, cut] = (
                residual[v, :, cut] - step * planes[v % ANGLES, j, pl.ds(first, detector_rows), :]
            )
        out_copy(v).start()
    gradient = residual_part[...] - step * image_part[...]
    gradient_next[...] = gradient
    solution_next[...] = solution[...] + step * direction[...]
    direction_next[...] = gradient + beta * direction[...]
    for v in range(views):
        out_copy(v).wait()


def summed_over_slabs(x):
    count = lax.axis_size("slab")
    for mask in (1, 2, 4, 8, 16):
        x = x + lax.ppermute(x, "slab", [(i, i ^ mask) for i in range(count)])
    return x


def local(solution, direction, gradient, residual, tiles, offsets):
    slab_rows, cells = solution.shape
    views, detector_rows, columns = residual.shape
    near = 3 * slab_rows
    blocks = columns // LANES
    count = lax.axis_size("slab")
    pair = [(i, i ^ 1) for i in range(count)]
    cross = [(i, i + 1) for i in range(1, count - 1, 2)]
    cross = cross + [(i, j) for j, i in cross]

    vmem = pl.BlockSpec(memory_space=pltpu.VMEM)
    smem = pl.BlockSpec(memory_space=pltpu.SMEM)
    anywhere = pl.BlockSpec(memory_space=pl.ANY)
    sds = jax.ShapeDtypeStruct

    direction_pair = lax.ppermute(direction, "slab", pair)
    direction_cross = lax.ppermute(direction, "slab", cross)

    wide = cells + LANES
    tiles_here, own, to_pair, to_cross, residual_here = pl.pallas_call(
        backproject_residual,
        name="backproject_residual",
        in_specs=[smem, anywhere, anywhere],
        out_specs=[vmem] * 5,
        out_shape=[
            pltpu.VMEM(tiles.shape, BF16),
            sds((slab_rows, wide), F32),
            sds((slab_rows, wide), BF16),
            sds((slab_rows, wide), BF16),
            pltpu.VMEM(residual.shape, F32),
        ],
        scratch_shapes=[
            pltpu.VMEM((blocks, near, LANES), F32),
            pltpu.VMEM((near, wide), F32),
            pltpu.SemaphoreType.DMA((views,)),
            pltpu.SemaphoreType.DMA((ANGLES * 2,)),
        ],
        compiler_params=pltpu.CompilerParams(vmem_limit_bytes=40 * MIB),
        cost_estimate=pl.CostEstimate(
            flops=4 * near * cells * columns * ANGLES, bytes_accessed=20 * MIB, transcendentals=0
        ),
    )(offsets, residual, tiles)

    from_pair = lax.ppermute(to_pair, "slab", pair)
    from_cross = lax.ppermute(to_cross, "slab", cross)

    planes, back, squares, grad_sums = pl.pallas_call(
        project_planes,
        name="project_planes",
        in_specs=[vmem] * 5,
        out_specs=[vmem] * 4,
        out_shape=[
            sds((ANGLES, blocks, near, LANES), F32),
            sds((ANGLES, slab_rows, cells), F32),
            sds((ANGLES, slab_rows, LANES), F32),
            sds((1, LANES), F32),
        ],
        scratch_shapes=[pltpu.VMEM((near, cells), BF16)],
        compiler_params=pltpu.CompilerParams(vmem_limit_bytes=40 * MIB),
        cost_estimate=pl.CostEstimate(
            flops=5 * near * cells * columns * ANGLES, bytes_accessed=4 * MIB, transcendentals=0
        ),
    )(direction, direction_pair, direction_cross, gradient, tiles_here)

    residual_part, image_part, sums = pl.pallas_call(
        combine,
        name="combine",
        in_specs=[vmem] * 6,
        out_specs=[vmem] * 3,
        out_shape=[
            sds((slab_rows, cells), F32),
            sds((slab_rows, cells), F32),
            sds((8, LANES), F32),
        ],
        compiler_params=pltpu.CompilerParams(vmem_limit_bytes=24 * MIB),
    )(own, from_pair, from_cross, back, squares, grad_sums)

    sums = summed_over_slabs(sums)

    return pl.pallas_call(
        finish,
        name="finish",
        in_specs=[smem] + [vmem] * 7,
        out_specs=[vmem, anywhere, vmem, vmem],
        out_shape=[
            sds(solution.shape, F32),
            sds(residual.shape, F32),
            sds(solution.shape, F32),
            sds(solution.shape, F32),
        ],
        scratch_shapes=[
            pltpu.VMEM(residual.shape, F32),
            pltpu.SemaphoreType.DMA((views,)),
        ],
        compiler_params=pltpu.CompilerParams(vmem_limit_bytes=32 * MIB),
    )(offsets, sums, solution, direction, residual_part, image_part, planes, residual_here)


def solution(mesh):
    placed = (
        P(("scan", "slab"), None),
        P(("scan", "slab"), None),
        P(("scan", "slab"), None),
        P(("scan", "slab"), None, None),
        P(),
        P(("scan", "slab")),
    )
    return jax.shard_map(
        local,
        mesh=mesh,
        in_specs=placed,
        out_specs=(
            P(("scan", "slab"), None),
            P(("scan", "slab"), None, None),
            P(("scan", "slab"), None),
            P(("scan", "slab"), None),
        ),
        check_vma=False,
    )
```

```python
import jax
import jax.numpy as jnp
from jax import lax
from jax.experimental import pallas as pl
from jax.experimental.pallas import tpu as pltpu
from jax.sharding import PartitionSpec as P

ANGLES = 4
LANES = 128
F32 = jnp.float32
BF16 = jnp.bfloat16
MIB = 1 << 20


def first_plane(offsets, v, slab_rows):
    return offsets[v] - lax.axis_index("slab") * slab_rows + slab_rows


def pair_is_above():
    return lax.rem(lax.axis_index("slab"), 2) == 0


def split(x):
    high = x.astype(BF16)
    return high, (x - high.astype(F32)).astype(BF16)


def lane_sums(x):
    total = x[:, :LANES]
    for j in range(1, x.shape[1] // LANES):
        total = total + x[:, j * LANES : (j + 1) * LANES]
    return jnp.sum(total, axis=0, keepdims=True)


def backproject_residual(offsets, residual_hbm, tiles_hbm, tiles, own, to_pair, to_cross,
                         residual, rows, acc, residual_sem, tiles_sem):
    views, detector_rows, columns = residual.shape
    slab_rows, cells = own.shape[0], tiles.shape[1]
    near = 3 * slab_rows
    blocks = columns // LANES
    parts = 2
    part_cells = cells // parts

    def residual_copy(v):
        return pltpu.make_async_copy(residual_hbm.at[v], residual.at[v], residual_sem.at[v])

    def tile_copy(a, h):
        cut = pl.ds(h * part_cells, part_cells)
        return pltpu.make_async_copy(
            tiles_hbm.at[a, cut], tiles.at[a, cut], tiles_sem.at[a * parts + h]
        )

    order = [g * ANGLES + a for a in range(ANGLES) for g in range(views // ANGLES)]
    for v in order:
        residual_copy(v).start()
    for a in range(ANGLES):
        for h in range(parts):
            tile_copy(a, h).start()

    rows[...] = jnp.zeros_like(rows)
    plane = lax.broadcasted_iota(jnp.int32, (near, LANES), 0)
    lane = lax.broadcasted_iota(jnp.int32, (near, LANES), 1)
    counts = jnp.zeros((near, LANES), F32)
    for v in range(views):
        first = first_plane(offsets, v, slab_rows)
        seen = (plane >= first) & (plane < first + detector_rows) & (lane == v % ANGLES)
        counts = counts + seen.astype(F32)
    acc[:, cells:] = counts

    for a in range(ANGLES):
        for g in range(views // ANGLES):
            v = g * ANGLES + a
            first = first_plane(offsets, v, slab_rows)
            residual_copy(v).wait()
            for j in range(blocks):
                rows[j, pl.ds(first, detector_rows), :] += residual[
                    v, :, j * LANES : (j + 1) * LANES
                ]
        summed = jnp.concatenate([rows[j] for j in range(blocks)], axis=1)
        if a + 1 < ANGLES:
            rows[...] = jnp.zeros_like(rows)
        both = jnp.concatenate(split(summed), axis=0)
        for h in range(parts):
            tile_copy(a, h).wait()
            for b in range(h * part_cells, (h + 1) * part_cells, 512):
                part = lax.dot_general(
                    both, tiles[a, b : b + 512, :], (((1,), (1,)), ((), ())),
                    preferred_element_type=F32,
                )
                part = part[:near] + part[near:]
                if a == 0:
                    acc[:, b : b + 512] = part
                else:
                    acc[:, b : b + 512] += part

    own[...] = acc[slab_rows : 2 * slab_rows, :]
    above = pair_is_above()
    pair_row = pl.multiple_of(jnp.where(above, 2 * slab_rows, 0), 16)
    cross_row = pl.multiple_of(jnp.where(above, 0, 2 * slab_rows), 16)
    to_pair[...] = acc[pl.ds(pair_row, slab_rows), :].astype(BF16)
    to_cross[...] = acc[pl.ds(cross_row, slab_rows), :].astype(BF16)


def project_planes(direction, from_pair, from_cross, gradient, tiles, planes, back, squares,
                   grad_sums, near):
    slab_rows = direction.shape[0]
    columns = tiles.shape[2]
    above = pair_is_above()
    pair_row = pl.multiple_of(jnp.where(above, 2 * slab_rows, 0), 16)
    cross_row = pl.multiple_of(jnp.where(above, 0, 2 * slab_rows), 16)
    near[pl.ds(slab_rows, slab_rows), :] = direction[...].astype(BF16)
    near[pl.ds(pair_row, slab_rows), :] = from_pair[...].astype(BF16)
    near[pl.ds(cross_row, slab_rows), :] = from_cross[...].astype(BF16)
    grad_sums[...] = lane_sums(gradient[...] * gradient[...])
    for a in range(ANGLES):
        image = jnp.dot(near[...], tiles[a], preferred_element_type=F32)
        total = None
        for j in range(columns // LANES):
            block = image[:, j * LANES : (j + 1) * LANES]
            planes[a, j] = block
            mine = block[slab_rows : 2 * slab_rows]
            total = mine * mine if total is None else total + mine * mine
        squares[a] = total
        both = jnp.concatenate(split(image[slab_rows : 2 * slab_rows]), axis=0)
        for b in range(0, tiles.shape[1], 512):
            part = lax.dot_general(
                both, tiles[a, b : b + 512, :], (((1,), (1,)), ((), ())),
                preferred_element_type=F32,
            )
            back[a, :, b : b + 512] = part[:slab_rows] + part[slab_rows:]


def combine(own, from_pair, from_cross, back, squares, grad_sums, residual_part, image_part, sums):
    cells = residual_part.shape[1]
    counts = own[:, cells:] + from_pair[:, cells:].astype(F32) + from_cross[:, cells:].astype(F32)
    zero = jnp.zeros((1, LANES), F32)
    rr, ri, ii = zero, zero, zero
    weights = [counts[:, a : a + 1] for a in range(ANGLES)]
    for b in range(0, cells, 512):
        cut = slice(b, b + 512)
        r = own[:, cut] + from_pair[:, cut].astype(F32) + from_cross[:, cut].astype(F32)
        i = weights[0] * back[0, :, cut]
        for a in range(1, ANGLES):
            i = i + weights[a] * back[a, :, cut]
        residual_part[:, cut] = r
        image_part[:, cut] = i
        rr, ri, ii = rr + lane_sums(r * r), ri + lane_sums(r * i), ii + lane_sums(i * i)
    image_norm = weights[0] * squares[0]
    for a in range(1, ANGLES):
        image_norm = image_norm + weights[a] * squares[a]
    sums[...] = jnp.concatenate(
        [grad_sums[...], lane_sums(image_norm), rr, ri, ii, zero, zero, zero], axis=0
    )


def finish(offsets, sums, solution, direction, residual_part, image_part, planes, residual,
           solution_next, residual_hbm, gradient_next, direction_next, updated, sem):
    views, detector_rows, columns = residual.shape
    slab_rows = solution.shape[0]
    total = jnp.sum(sums[...], axis=1, keepdims=True)
    grad_norm, image_norm = total[0:1], total[1:2]
    step = grad_norm / image_norm
    new_norm = total[2:3] - 2.0 * step * total[3:4] + step * step * total[4:5]
    beta = new_norm / grad_norm

    def out_copy(v):
        return pltpu.make_async_copy(updated.at[v], residual_hbm.at[v], sem.at[v])

    for v in range(views):
        first = first_plane(offsets, v, slab_rows)
        for j in range(columns // LANES):
            cut = slice(j * LANES, (j + 1) * LANES)
            updated[v, :, cut] = (
                residual[v, :, cut] - step * planes[v % ANGLES, j, pl.ds(first, detector_rows), :]
            )
        out_copy(v).start()
    gradient = residual_part[...] - step * image_part[...]
    gradient_next[...] = gradient
    solution_next[...] = solution[...] + step * direction[...]
    direction_next[...] = gradient + beta * direction[...]
    for v in range(views):
        out_copy(v).wait()


def summed_over_slabs(x):
    count = lax.axis_size("slab")
    for mask in (1, 2, 4, 8, 16):
        x = x + lax.ppermute(x, "slab", [(i, i ^ mask) for i in range(count)])
    return x


def local(solution, direction, gradient, residual, tiles, offsets):
    slab_rows, cells = solution.shape
    views, detector_rows, columns = residual.shape
    near = 3 * slab_rows
    blocks = columns // LANES
    count = lax.axis_size("slab")
    pair = [(i, i ^ 1) for i in range(count)]
    cross = [(i, i + 1) for i in range(1, count - 1, 2)]
    cross = cross + [(i, j) for j, i in cross]

    vmem = pl.BlockSpec(memory_space=pltpu.VMEM)
    smem = pl.BlockSpec(memory_space=pltpu.SMEM)
    hbm = pl.BlockSpec(memory_space=pltpu.HBM)
    sds = jax.ShapeDtypeStruct

    direction_pair = lax.ppermute(direction, "slab", pair)
    direction_cross = lax.ppermute(direction, "slab", cross)

    wide = cells + LANES
    tiles_here, own, to_pair, to_cross, residual_here = pl.pallas_call(
        backproject_residual,
        name="backproject_residual",
        in_specs=[smem, hbm, hbm],
        out_specs=[vmem] * 5,
        out_shape=[
            pltpu.VMEM(tiles.shape, BF16),
            sds((slab_rows, wide), F32),
            sds((slab_rows, wide), BF16),
            sds((slab_rows, wide), BF16),
            pltpu.VMEM(residual.shape, F32),
        ],
        scratch_shapes=[
            pltpu.VMEM((blocks, near, LANES), F32),
            pltpu.VMEM((near, wide), F32),
            pltpu.SemaphoreType.DMA((views,)),
            pltpu.SemaphoreType.DMA((ANGLES * 2,)),
        ],
        compiler_params=pltpu.CompilerParams(vmem_limit_bytes=20 * MIB),
        cost_estimate=pl.CostEstimate(
            flops=4 * near * cells * columns * ANGLES, bytes_accessed=20 * MIB, transcendentals=0
        ),
    )(offsets, residual, tiles)

    from_pair = lax.ppermute(to_pair, "slab", pair)
    from_cross = lax.ppermute(to_cross, "slab", cross)

    planes, back, squares, grad_sums = pl.pallas_call(
        project_planes,
        name="project_planes",
        in_specs=[vmem] * 5,
        out_specs=[vmem] * 4,
        out_shape=[
            sds((ANGLES, blocks, near, LANES), F32),
            sds((ANGLES, slab_rows, cells), F32),
            sds((ANGLES, slab_rows, LANES), F32),
            sds((1, LANES), F32),
        ],
        scratch_shapes=[pltpu.VMEM((near, cells), BF16)],
        compiler_params=pltpu.CompilerParams(vmem_limit_bytes=12 * MIB),
        cost_estimate=pl.CostEstimate(
            flops=5 * near * cells * columns * ANGLES, bytes_accessed=4 * MIB, transcendentals=0
        ),
    )(direction, direction_pair, direction_cross, gradient, tiles_here)

    residual_part, image_part, sums = pl.pallas_call(
        combine,
        name="combine",
        in_specs=[vmem] * 6,
        out_specs=[vmem] * 3,
        out_shape=[
            sds((slab_rows, cells), F32),
            sds((slab_rows, cells), F32),
            sds((8, LANES), F32),
        ],
        compiler_params=pltpu.CompilerParams(vmem_limit_bytes=8 * MIB),
    )(own, from_pair, from_cross, back, squares, grad_sums)

    sums = summed_over_slabs(sums)

    return pl.pallas_call(
        finish,
        name="finish",
        in_specs=[smem] + [vmem] * 7,
        out_specs=[vmem, hbm, vmem, vmem],
        out_shape=[
            sds(solution.shape, F32),
            sds(residual.shape, F32),
            sds(solution.shape, F32),
            sds(solution.shape, F32),
        ],
        scratch_shapes=[
            pltpu.VMEM(residual.shape, F32),
            pltpu.SemaphoreType.DMA((views,)),
        ],
        compiler_params=pltpu.CompilerParams(vmem_limit_bytes=12 * MIB),
    )(offsets, sums, solution, direction, residual_part, image_part, planes, residual_here)


def solution(mesh):
    placed = (
        P(("scan", "slab"), None),
        P(("scan", "slab"), None),
        P(("scan", "slab"), None),
        P(("scan", "slab"), None, None),
        P(),
        P(("scan", "slab")),
    )
    return jax.shard_map(
        local,
        mesh=mesh,
        in_specs=placed,
        out_specs=(
            P(("scan", "slab"), None),
            P(("scan", "slab"), None, None),
            P(("scan", "slab"), None),
            P(("scan", "slab"), None),
        ),
        check_vma=False,
    )
```

```python
import jax
import jax.numpy as jnp
from jax import lax
from jax.experimental import pallas as pl
from jax.experimental.pallas import tpu as pltpu
from jax.sharding import PartitionSpec as P

ANGLES = 4
LANES = 128
F32 = jnp.float32
BF16 = jnp.bfloat16
MIB = 1 << 20


def first_plane(offsets, v, slab_rows):
    return offsets[v] - lax.axis_index("slab") * slab_rows + slab_rows


def pair_is_above():
    return lax.rem(lax.axis_index("slab"), 2) == 0


def split(x):
    high = x.astype(BF16)
    return high, (x - high.astype(F32)).astype(BF16)


def lane_sums(x):
    total = x[:, :LANES]
    for j in range(1, x.shape[1] // LANES):
        total = total + x[:, j * LANES : (j + 1) * LANES]
    return jnp.sum(total, axis=0, keepdims=True)


def sum_residuals(offsets_hbm, residual_hbm, tiles_hbm, own, to_pair, to_cross, residual, tile,
                  rows, offsets, sem, offsets_sem, tile_sem):
    views, detector_rows, columns = residual.shape
    slab_rows = own.shape[0]
    near = 3 * slab_rows
    blocks = columns // LANES

    def copy(v):
        return pltpu.make_async_copy(residual_hbm.at[v], residual.at[v], sem.at[v])

    offsets_copy = pltpu.make_async_copy(offsets_hbm, offsets, offsets_sem)
    offsets_copy.start()
    for v in range(views):
        copy(v).start()
    tile_copy = pltpu.make_async_copy(tiles_hbm.at[0], tile, tile_sem)
    tile_copy.start()
    above = pair_is_above()
    pair_row = pl.multiple_of(jnp.where(above, 2 * slab_rows, 0), 16)
    cross_row = pl.multiple_of(jnp.where(above, 0, 2 * slab_rows), 16)

    rows[: ANGLES * blocks] = jnp.zeros((ANGLES * blocks, near, LANES), F32)
    plane = lax.broadcasted_iota(jnp.int32, (near, LANES), 0)
    lane = lax.broadcasted_iota(jnp.int32, (near, LANES), 1)
    counts = jnp.zeros((near, LANES), F32)
    offsets_copy.wait()
    for v in range(views):
        first = first_plane(offsets, v, slab_rows)
        seen = (plane >= first) & (plane < first + detector_rows) & (lane == v % ANGLES)
        counts = counts + seen.astype(F32)
    rows[ANGLES * blocks] = counts

    for v in range(views):
        first = first_plane(offsets, v, slab_rows)
        copy(v).wait()
        for j in range(blocks):
            rows[v % ANGLES * blocks + j, pl.ds(first, detector_rows), :] += residual[
                v, :, j * LANES : (j + 1) * LANES
            ]
    for k in range(ANGLES * blocks + 1):
        cut = slice(k * LANES, (k + 1) * LANES)
        to_pair[:, cut] = rows[k, pl.ds(pair_row, slab_rows), :].astype(BF16)
        to_cross[:, cut] = rows[k, pl.ds(cross_row, slab_rows), :].astype(BF16)
        own[:, cut] = rows[k, slab_rows : 2 * slab_rows, :]
    tile_copy.wait()


def project_planes(direction, from_pair, from_cross, gradient, tile, tiles_hbm, planes, back,
                   squares, grad_sums, tiles, near, sem):
    slab_rows = direction.shape[0]
    cells, columns = tile.shape
    copies = [
        pltpu.make_async_copy(tiles_hbm.at[a], tiles.at[a - 1], sem.at[a - 1])
        for a in range(1, ANGLES)
    ]
    for c in copies:
        c.start()
    above = pair_is_above()
    pair_row = pl.multiple_of(jnp.where(above, 2 * slab_rows, 0), 16)
    cross_row = pl.multiple_of(jnp.where(above, 0, 2 * slab_rows), 16)
    near[pl.ds(slab_rows, slab_rows), :] = direction[...].astype(BF16)
    near[pl.ds(pair_row, slab_rows), :] = from_pair[...].astype(BF16)
    near[pl.ds(cross_row, slab_rows), :] = from_cross[...].astype(BF16)
    grad_sums[...] = lane_sums(gradient[...] * gradient[...])
    for a in range(ANGLES):
        weights = tile if a == 0 else tiles.at[a - 1]
        if a > 0:
            copies[a - 1].wait()
        image = jnp.dot(near[...], weights[...], preferred_element_type=F32)
        total = None
        for j in range(columns // LANES):
            block = image[:, j * LANES : (j + 1) * LANES]
            planes[a, j] = block
            mine = block[slab_rows : 2 * slab_rows]
            total = mine * mine if total is None else total + mine * mine
        squares[a] = total
        both = jnp.concatenate(split(image[slab_rows : 2 * slab_rows]), axis=0)
        for b in range(0, cells, 512):
            part = lax.dot_general(
                both, weights[b : b + 512, :], (((1,), (1,)), ((), ())),
                preferred_element_type=F32,
            )
            back[a, :, b : b + 512] = part[:slab_rows] + part[slab_rows:]


def combine(own, from_pair, from_cross, tile, tiles, back, squares, grad_sums, residual_part,
            image_part, sums):
    slab_rows = own.shape[0]
    cells, columns = tile.shape

    def gathered(cut):
        return own[:, cut] + from_pair[:, cut].astype(F32) + from_cross[:, cut].astype(F32)

    for a in range(ANGLES):
        rows = gathered(slice(a * columns, (a + 1) * columns))
        both = jnp.concatenate(split(rows), axis=0)
        weights = tile if a == 0 else tiles.at[a - 1]
        for b in range(0, cells, 512):
            part = lax.dot_general(
                both, weights[b : b + 512, :], (((1,), (1,)), ((), ())),
                preferred_element_type=F32,
            )
            part = part[:slab_rows] + part[slab_rows:]
            if a == 0:
                residual_part[:, b : b + 512] = part
            else:
                residual_part[:, b : b + 512] += part

    counts = gathered(slice(ANGLES * columns, ANGLES * columns + LANES))
    zero = jnp.zeros((1, LANES), F32)
    rr, ri, ii = zero, zero, zero
    weights = [counts[:, a : a + 1] for a in range(ANGLES)]
    for b in range(0, cells, 512):
        cut = slice(b, b + 512)
        r = residual_part[:, cut]
        i = weights[0] * back[0, :, cut]
        for a in range(1, ANGLES):
            i = i + weights[a] * back[a, :, cut]
        image_part[:, cut] = i
        rr, ri, ii = rr + lane_sums(r * r), ri + lane_sums(r * i), ii + lane_sums(i * i)
    image_norm = weights[0] * squares[0]
    for a in range(1, ANGLES):
        image_norm = image_norm + weights[a] * squares[a]
    sums[...] = jnp.concatenate(
        [grad_sums[...], lane_sums(image_norm), rr, ri, ii, zero, zero, zero], axis=0
    )


def finish(offsets, sums, solution, direction, residual_part, image_part, planes, residual,
           solution_hbm, residual_hbm, gradient_hbm, direction_hbm, updated, small, sem, small_sem):
    views, detector_rows, columns = residual.shape
    slab_rows = solution.shape[0]
    total = jnp.sum(sums[...], axis=1, keepdims=True)
    grad_norm, image_norm = total[0:1], total[1:2]
    step = grad_norm / image_norm
    new_norm = total[2:3] - 2.0 * step * total[3:4] + step * step * total[4:5]
    beta = new_norm / grad_norm

    def out_copy(v):
        return pltpu.make_async_copy(updated.at[v], residual_hbm.at[v], sem.at[v])

    small_copies = [
        pltpu.make_async_copy(small.at[k], target, small_sem.at[k])
        for k, target in enumerate((gradient_hbm, solution_hbm, direction_hbm))
    ]
    gradient = residual_part[...] - step * image_part[...]
    small[0] = gradient
    small_copies[0].start()
    small[1] = solution[...] + step * direction[...]
    small_copies[1].start()
    small[2] = gradient + beta * direction[...]
    small_copies[2].start()
    for v in range(views):
        first = first_plane(offsets, v, slab_rows)
        for j in range(columns // LANES):
            cut = slice(j * LANES, (j + 1) * LANES)
            updated[v, :, cut] = (
                residual[v, :, cut] - step * planes[v % ANGLES, j, pl.ds(first, detector_rows), :]
            )
        out_copy(v).start()
    for c in small_copies:
        c.wait()
    for v in range(views):
        out_copy(v).wait()


def summed_over_slabs(x):
    count = lax.axis_size("slab")
    for masks in ((1, 2, 3), (8, 16, 24), (4,)):
        terms = [lax.ppermute(x, "slab", [(i, i ^ m) for i in range(count)]) for m in masks]
        for term in terms:
            x = x + term
    return x


def local(solution, direction, gradient, residual, tiles, offsets):
    slab_rows, cells = solution.shape
    views, detector_rows, columns = residual.shape
    near = 3 * slab_rows
    blocks = columns // LANES
    count = lax.axis_size("slab")
    pair = [(i, i ^ 1) for i in range(count)]
    cross = [(i, i + 1) for i in range(1, count - 1, 2)]
    cross = cross + [(i, j) for j, i in cross]

    vmem = pl.BlockSpec(memory_space=pltpu.VMEM)
    smem = pl.BlockSpec(memory_space=pltpu.SMEM)
    hbm = pl.BlockSpec(memory_space=pltpu.HBM)
    sds = jax.ShapeDtypeStruct

    direction_cross = lax.ppermute(direction, "slab", cross)
    direction_pair = lax.ppermute(direction, "slab", pair)

    wide = ANGLES * columns + LANES
    tiles = pltpu.with_memory_space_constraint(tiles, pltpu.HBM)
    own, to_pair, to_cross, residual_here, tile = pl.pallas_call(
        sum_residuals,
        name="sum_residuals",
        in_specs=[hbm] * 3,
        out_specs=[vmem] * 5,
        out_shape=[
            sds((slab_rows, wide), F32),
            sds((slab_rows, wide), BF16),
            sds((slab_rows, wide), BF16),
            pltpu.VMEM(residual.shape, F32),
            pltpu.VMEM(tiles.shape[1:], BF16),
        ],
        scratch_shapes=[
            pltpu.VMEM((wide // LANES, near, LANES), F32),
            pltpu.SMEM(offsets.shape, jnp.int32),
            pltpu.SemaphoreType.DMA((views,)),
            pltpu.SemaphoreType.DMA,
            pltpu.SemaphoreType.DMA,
        ],
        compiler_params=pltpu.CompilerParams(vmem_limit_bytes=8 * MIB),
        cost_estimate=pl.CostEstimate(
            flops=residual.size, bytes_accessed=4 * residual.size, transcendentals=0
        ),
    )(
        pltpu.with_memory_space_constraint(offsets, pltpu.HBM),
        pltpu.with_memory_space_constraint(residual, pltpu.HBM),
        tiles,
    )

    from_cross = lax.ppermute(to_cross, "slab", cross)
    from_pair = lax.ppermute(to_pair, "slab", pair)

    planes, back, squares, grad_sums, tiles_here = pl.pallas_call(
        project_planes,
        name="project_planes",
        in_specs=[vmem] * 5 + [hbm],
        out_specs=[vmem] * 5,
        out_shape=[
            sds((ANGLES, blocks, near, LANES), F32),
            sds((ANGLES, slab_rows, cells), F32),
            sds((ANGLES, slab_rows, LANES), F32),
            sds((1, LANES), F32),
            pltpu.VMEM((ANGLES - 1, *tiles.shape[1:]), BF16),
        ],
        scratch_shapes=[
            pltpu.VMEM((near, cells), BF16),
            pltpu.SemaphoreType.DMA((ANGLES - 1,)),
        ],
        compiler_params=pltpu.CompilerParams(vmem_limit_bytes=8 * MIB),
        cost_estimate=pl.CostEstimate(
            flops=5 * near * cells * columns * ANGLES, bytes_accessed=4 * MIB, transcendentals=0
        ),
    )(direction, direction_pair, direction_cross, gradient, tile, tiles)

    residual_part, image_part, sums = pl.pallas_call(
        combine,
        name="combine",
        in_specs=[vmem] * 8,
        out_specs=[vmem] * 3,
        out_shape=[
            sds((slab_rows, cells), F32),
            sds((slab_rows, cells), F32),
            sds((8, LANES), F32),
        ],
        compiler_params=pltpu.CompilerParams(vmem_limit_bytes=8 * MIB),
    )(own, from_pair, from_cross, tile, tiles_here, back, squares, grad_sums)

    sums = summed_over_slabs(sums)

    return pl.pallas_call(
        finish,
        name="finish",
        in_specs=[smem] + [vmem] * 7,
        out_specs=[hbm] * 4,
        out_shape=[
            sds(solution.shape, F32),
            sds(residual.shape, F32),
            sds(solution.shape, F32),
            sds(solution.shape, F32),
        ],
        scratch_shapes=[
            pltpu.VMEM(residual.shape, F32),
            pltpu.VMEM((3, slab_rows, cells), F32),
            pltpu.SemaphoreType.DMA((views,)),
            pltpu.SemaphoreType.DMA((3,)),
        ],
        compiler_params=pltpu.CompilerParams(vmem_limit_bytes=12 * MIB),
    )(offsets, sums, solution, direction, residual_part, image_part, planes, residual_here)


def solution(mesh):
    placed = (
        P(("scan", "slab"), None),
        P(("scan", "slab"), None),
        P(("scan", "slab"), None),
        P(("scan", "slab"), None, None),
        P(),
        P(("scan", "slab")),
    )
    return jax.shard_map(
        local,
        mesh=mesh,
        in_specs=placed,
        out_specs=(
            P(("scan", "slab"), None),
            P(("scan", "slab"), None, None),
            P(("scan", "slab"), None),
            P(("scan", "slab"), None),
        ),
        check_vma=False,
    )
```

```python
import jax
import jax.numpy as jnp
from jax import lax
from jax.experimental import pallas as pl
from jax.experimental.pallas import tpu as pltpu
from jax.sharding import PartitionSpec as P

ANGLES = 4
LANES = 128
CHUNK = 512
F32 = jnp.float32
BF16 = jnp.bfloat16
MIB = 1 << 20


def first_plane(offsets, v, slab_rows):
    return offsets[v] - lax.axis_index("slab") * slab_rows + slab_rows


def pair_is_above():
    return lax.rem(lax.axis_index("slab"), 2) == 0


def split(x):
    high = x.astype(BF16)
    return high, (x - high.astype(F32)).astype(BF16)


def lane_sums(x):
    total = x[:, :LANES]
    for j in range(1, x.shape[1] // LANES):
        total = total + x[:, j * LANES : (j + 1) * LANES]
    return jnp.sum(total, axis=0, keepdims=True)


def sum_residuals(offsets_hbm, residual_hbm, tiles_hbm, own, to_pair, to_cross, residual, tile,
                  rows, offsets, sem, offsets_sem, tile_sem):
    views, detector_rows, columns = residual.shape
    slab_rows = own.shape[0]
    near = 3 * slab_rows
    blocks = columns // LANES

    def copy(v):
        return pltpu.make_async_copy(residual_hbm.at[v], residual.at[v], sem.at[v])

    offsets_copy = pltpu.make_async_copy(offsets_hbm, offsets, offsets_sem)
    offsets_copy.start()
    for v in range(views):
        copy(v).start()
    tile_copy = pltpu.make_async_copy(tiles_hbm.at[0], tile, tile_sem)
    tile_copy.start()
    above = pair_is_above()
    pair_row = pl.multiple_of(jnp.where(above, 2 * slab_rows, 0), 16)
    cross_row = pl.multiple_of(jnp.where(above, 0, 2 * slab_rows), 16)

    rows[: ANGLES * blocks] = jnp.zeros((ANGLES * blocks, near, LANES), F32)
    plane = lax.broadcasted_iota(jnp.int32, (near, LANES), 0)
    lane = lax.broadcasted_iota(jnp.int32, (near, LANES), 1)
    counts = jnp.zeros((near, LANES), F32)
    offsets_copy.wait()
    for v in range(views):
        first = first_plane(offsets, v, slab_rows)
        seen = (plane >= first) & (plane < first + detector_rows) & (lane == v % ANGLES)
        counts = counts + seen.astype(F32)
    rows[ANGLES * blocks] = counts

    for v in range(views):
        first = first_plane(offsets, v, slab_rows)
        copy(v).wait()
        for j in range(blocks):
            rows[v % ANGLES * blocks + j, pl.ds(first, detector_rows), :] += residual[
                v, :, j * LANES : (j + 1) * LANES
            ]
    for k in range(ANGLES * blocks + 1):
        cut = slice(k * LANES, (k + 1) * LANES)
        to_pair[:, cut] = rows[k, pl.ds(pair_row, slab_rows), :].astype(BF16)
        to_cross[:, cut] = rows[k, pl.ds(cross_row, slab_rows), :].astype(BF16)
        own[:, cut] = rows[k, slab_rows : 2 * slab_rows, :]
    tile_copy.wait()


def project_planes(direction, from_pair, from_cross, gradient, tile, tiles_hbm, planes, grad_sums,
                   tiles, near, sem):
    slab_rows = direction.shape[0]
    columns = tile.shape[1]
    copies = [
        pltpu.make_async_copy(tiles_hbm.at[a], tiles.at[a - 1], sem.at[a - 1])
        for a in range(1, ANGLES)
    ]
    for c in copies:
        c.start()
    above = pair_is_above()
    pair_row = pl.multiple_of(jnp.where(above, 2 * slab_rows, 0), 16)
    cross_row = pl.multiple_of(jnp.where(above, 0, 2 * slab_rows), 16)
    near[pl.ds(slab_rows, slab_rows), :] = direction[...].astype(BF16)
    near[pl.ds(pair_row, slab_rows), :] = from_pair[...].astype(BF16)
    near[pl.ds(cross_row, slab_rows), :] = from_cross[...].astype(BF16)
    grad_sums[...] = lane_sums(gradient[...] * gradient[...])
    for a in range(ANGLES):
        weights = tile if a == 0 else tiles.at[a - 1]
        if a > 0:
            copies[a - 1].wait()
        image = jnp.dot(near[...], weights[...], preferred_element_type=F32)
        for j in range(columns // LANES):
            planes[a, j] = image[:, j * LANES : (j + 1) * LANES]


def combine(own, from_pair, from_cross, tile, tiles, planes, grad_sums, residual_part, image_part,
            sums):
    slab_rows = own.shape[0]
    cells, columns = tile.shape
    zero = jnp.zeros((1, LANES), F32)

    def gathered(cut):
        return own[:, cut] + from_pair[:, cut].astype(F32) + from_cross[:, cut].astype(F32)

    counts = gathered(slice(ANGLES * columns, ANGLES * columns + LANES))
    image_norm = zero
    for a in range(ANGLES):
        rows = gathered(slice(a * columns, (a + 1) * columns))
        image = jnp.concatenate(
            [planes[a, j, slab_rows : 2 * slab_rows, :] for j in range(columns // LANES)], axis=1
        )
        weighted = counts[:, a : a + 1] * image
        image_norm = image_norm + lane_sums(weighted * image)
        both = jnp.concatenate([*split(rows), *split(weighted)], axis=0)
        weights = tile if a == 0 else tiles.at[a - 1]
        for b in range(0, cells, CHUNK):
            cut = slice(b, b + CHUNK)
            part = lax.dot_general(
                both, weights[cut, :], (((1,), (1,)), ((), ())), preferred_element_type=F32
            )
            r = part[:slab_rows] + part[slab_rows : 2 * slab_rows]
            i = part[2 * slab_rows : 3 * slab_rows] + part[3 * slab_rows :]
            if a == 0:
                residual_part[:, cut] = r
                image_part[:, cut] = i
            else:
                residual_part[:, cut] += r
                image_part[:, cut] += i

    rr, ri, ii = zero, zero, zero
    for b in range(0, cells, CHUNK):
        r, i = residual_part[:, b : b + CHUNK], image_part[:, b : b + CHUNK]
        rr, ri, ii = rr + lane_sums(r * r), ri + lane_sums(r * i), ii + lane_sums(i * i)
    sums[...] = jnp.concatenate(
        [grad_sums[...], image_norm, rr, ri, ii, zero, zero, zero], axis=0
    )


def finish(offsets, sums, solution, direction, residual_part, image_part, planes, residual,
           solution_hbm, residual_hbm, gradient_hbm, direction_hbm, updated, small, sem, small_sem):
    views, detector_rows, columns = residual.shape
    slab_rows = solution.shape[0]
    total = jnp.sum(sums[...], axis=1, keepdims=True)
    grad_norm, image_norm = total[0:1], total[1:2]
    step = grad_norm / image_norm
    new_norm = total[2:3] - 2.0 * step * total[3:4] + step * step * total[4:5]
    beta = new_norm / grad_norm

    def out_copy(v):
        return pltpu.make_async_copy(updated.at[v], residual_hbm.at[v], sem.at[v])

    small_copies = [
        pltpu.make_async_copy(small.at[k], target, small_sem.at[k])
        for k, target in enumerate((gradient_hbm, solution_hbm, direction_hbm))
    ]
    gradient = residual_part[...] - step * image_part[...]
    small[0] = gradient
    small_copies[0].start()
    small[1] = solution[...] + step * direction[...]
    small_copies[1].start()
    small[2] = gradient + beta * direction[...]
    small_copies[2].start()
    for v in range(views):
        first = first_plane(offsets, v, slab_rows)
        for j in range(columns // LANES):
            cut = slice(j * LANES, (j + 1) * LANES)
            updated[v, :, cut] = (
                residual[v, :, cut] - step * planes[v % ANGLES, j, pl.ds(first, detector_rows), :]
            )
        out_copy(v).start()
    for c in small_copies:
        c.wait()
    for v in range(views):
        out_copy(v).wait()


def summed_over_slabs(x):
    count = lax.axis_size("slab")
    for masks in ((1, 2, 3), (8, 16, 24), (4,)):
        terms = [lax.ppermute(x, "slab", [(i, i ^ m) for i in range(count)]) for m in masks]
        for term in terms:
            x = x + term
    return x


def local(solution, direction, gradient, residual, tiles, offsets):
    slab_rows, cells = solution.shape
    views, detector_rows, columns = residual.shape
    near = 3 * slab_rows
    blocks = columns // LANES
    count = lax.axis_size("slab")
    pair = [(i, i ^ 1) for i in range(count)]
    cross = [(i, i + 1) for i in range(1, count - 1, 2)]
    cross = cross + [(i, j) for j, i in cross]

    vmem = pl.BlockSpec(memory_space=pltpu.VMEM)
    smem = pl.BlockSpec(memory_space=pltpu.SMEM)
    hbm = pl.BlockSpec(memory_space=pltpu.HBM)
    sds = jax.ShapeDtypeStruct

    direction_cross = lax.ppermute(direction, "slab", cross)
    direction_pair = lax.ppermute(direction, "slab", pair)

    wide = ANGLES * columns + LANES
    tiles = pltpu.with_memory_space_constraint(tiles, pltpu.HBM)
    own, to_pair, to_cross, residual_here, tile = pl.pallas_call(
        sum_residuals,
        name="sum_residuals",
        in_specs=[hbm] * 3,
        out_specs=[vmem] * 5,
        out_shape=[
            sds((slab_rows, wide), F32),
            sds((slab_rows, wide), BF16),
            sds((slab_rows, wide), BF16),
            pltpu.VMEM(residual.shape, F32),
            pltpu.VMEM(tiles.shape[1:], BF16),
        ],
        scratch_shapes=[
            pltpu.VMEM((wide // LANES, near, LANES), F32),
            pltpu.SMEM(offsets.shape, jnp.int32),
            pltpu.SemaphoreType.DMA((views,)),
            pltpu.SemaphoreType.DMA,
            pltpu.SemaphoreType.DMA,
        ],
        compiler_params=pltpu.CompilerParams(vmem_limit_bytes=8 * MIB),
        cost_estimate=pl.CostEstimate(
            flops=residual.size, bytes_accessed=4 * residual.size, transcendentals=0
        ),
    )(
        pltpu.with_memory_space_constraint(offsets, pltpu.HBM),
        pltpu.with_memory_space_constraint(residual, pltpu.HBM),
        tiles,
    )

    from_cross = lax.ppermute(to_cross, "slab", cross)
    from_pair = lax.ppermute(to_pair, "slab", pair)

    planes, grad_sums, tiles_here = pl.pallas_call(
        project_planes,
        name="project_planes",
        in_specs=[vmem] * 5 + [hbm],
        out_specs=[vmem] * 3,
        out_shape=[
            sds((ANGLES, blocks, near, LANES), F32),
            sds((1, LANES), F32),
            pltpu.VMEM((ANGLES - 1, *tiles.shape[1:]), BF16),
        ],
        scratch_shapes=[
            pltpu.VMEM((near, cells), BF16),
            pltpu.SemaphoreType.DMA((ANGLES - 1,)),
        ],
        compiler_params=pltpu.CompilerParams(vmem_limit_bytes=8 * MIB),
        cost_estimate=pl.CostEstimate(
            flops=2 * near * cells * columns * ANGLES, bytes_accessed=16 * MIB, transcendentals=0
        ),
    )(direction, direction_pair, direction_cross, gradient, tile, tiles)

    residual_part, image_part, sums = pl.pallas_call(
        combine,
        name="combine",
        in_specs=[vmem] * 7,
        out_specs=[vmem] * 3,
        out_shape=[
            sds((slab_rows, cells), F32),
            sds((slab_rows, cells), F32),
            sds((8, LANES), F32),
        ],
        compiler_params=pltpu.CompilerParams(vmem_limit_bytes=8 * MIB),
    )(own, from_pair, from_cross, tile, tiles_here, planes, grad_sums)

    sums = summed_over_slabs(sums)

    return pl.pallas_call(
        finish,
        name="finish",
        in_specs=[smem] + [vmem] * 7,
        out_specs=[hbm] * 4,
        out_shape=[
            sds(solution.shape, F32),
            sds(residual.shape, F32),
            sds(solution.shape, F32),
            sds(solution.shape, F32),
        ],
        scratch_shapes=[
            pltpu.VMEM(residual.shape, F32),
            pltpu.VMEM((3, slab_rows, cells), F32),
            pltpu.SemaphoreType.DMA((views,)),
            pltpu.SemaphoreType.DMA((3,)),
        ],
        compiler_params=pltpu.CompilerParams(vmem_limit_bytes=12 * MIB),
    )(offsets, sums, solution, direction, residual_part, image_part, planes, residual_here)


def solution(mesh):
    placed = (
        P(("scan", "slab"), None),
        P(("scan", "slab"), None),
        P(("scan", "slab"), None),
        P(("scan", "slab"), None, None),
        P(),
        P(("scan", "slab")),
    )
    return jax.shard_map(
        local,
        mesh=mesh,
        in_specs=placed,
        out_specs=(
            P(("scan", "slab"), None),
            P(("scan", "slab"), None, None),
            P(("scan", "slab"), None),
            P(("scan", "slab"), None),
        ),
        check_vma=False,
    )
```

```python
import functools

import jax
import jax.numpy as jnp
from jax import lax
from jax.experimental import pallas as pl
from jax.experimental.pallas import tpu as pltpu
from jax.sharding import PartitionSpec as P

ANGLES = 4
LANES = 128
CHUNK = 512
ROUNDS = ((1, 2, 3), (8, 16, 24), (4,))
GROUPS = ((0,), (1,), (2, 3))
F32 = jnp.float32
BF16 = jnp.bfloat16
MIB = 1 << 20


def first_plane(offsets, v, slab_rows):
    return offsets[v] - lax.axis_index("slab") * slab_rows + slab_rows


def pair_is_above():
    return lax.rem(lax.axis_index("slab"), 2) == 0


def split(x):
    high = x.astype(BF16)
    return high, (x - high.astype(F32)).astype(BF16)


def lane_sums(x):
    total = x[:, :LANES]
    for j in range(1, x.shape[1] // LANES):
        total = total + x[:, j * LANES : (j + 1) * LANES]
    return jnp.sum(total, axis=0, keepdims=True)


def sum_residuals(offsets_hbm, residual_hbm, tiles_hbm, direction_hbm, own, to_pair, to_cross,
                  residual, tile, half, rows, offsets, direction, sem, offsets_sem, tile_sem,
                  direction_sem):
    views, detector_rows, columns = residual.shape
    slab_rows = own.shape[0]
    near = 3 * slab_rows
    blocks = columns // LANES

    def copy(v):
        return pltpu.make_async_copy(residual_hbm.at[v], residual.at[v], sem.at[v])

    offsets_copy = pltpu.make_async_copy(offsets_hbm, offsets, offsets_sem)
    offsets_copy.start()
    for v in range(views):
        copy(v).start()
    direction_copy = pltpu.make_async_copy(direction_hbm, direction, direction_sem)
    direction_copy.start()
    tile_copy = pltpu.make_async_copy(tiles_hbm.at[0], tile, tile_sem)
    tile_copy.start()
    above = pair_is_above()
    pair_row = pl.multiple_of(jnp.where(above, 2 * slab_rows, 0), 16)
    cross_row = pl.multiple_of(jnp.where(above, 0, 2 * slab_rows), 16)

    rows[: ANGLES * blocks] = jnp.zeros((ANGLES * blocks, near, LANES), F32)
    plane = lax.broadcasted_iota(jnp.int32, (near, LANES), 0)
    lane = lax.broadcasted_iota(jnp.int32, (near, LANES), 1)
    counts = jnp.zeros((near, LANES), F32)
    offsets_copy.wait()
    for v in range(views):
        first = first_plane(offsets, v, slab_rows)
        seen = (plane >= first) & (plane < first + detector_rows) & (lane == v % ANGLES)
        counts = counts + seen.astype(F32)
    rows[ANGLES * blocks] = counts

    for v in range(views):
        first = first_plane(offsets, v, slab_rows)
        copy(v).wait()
        for j in range(blocks):
            rows[v % ANGLES * blocks + j, pl.ds(first, detector_rows), :] += residual[
                v, :, j * LANES : (j + 1) * LANES
            ]
    for k in range(ANGLES * blocks + 1):
        cut = slice(k * LANES, (k + 1) * LANES)
        to_pair[:, cut] = rows[k, pl.ds(pair_row, slab_rows), :].astype(BF16)
        to_cross[:, cut] = rows[k, pl.ds(cross_row, slab_rows), :].astype(BF16)
        own[:, cut] = rows[k, slab_rows : 2 * slab_rows, :]
    direction_copy.wait()
    half[...] = direction[...].astype(BF16)
    tile_copy.wait()


def project_own(half, gradient, tile, tiles_hbm, images, grad_sums, tiles, sem):
    copies = [
        pltpu.make_async_copy(tiles_hbm.at[a], tiles.at[a - 1], sem.at[a - 1])
        for a in range(1, ANGLES)
    ]
    for c in copies:
        c.start()
    grad_sums[...] = lane_sums(gradient[...] * gradient[...])
    images[0] = jnp.dot(half[...], tile[...], preferred_element_type=F32)
    for a in range(1, ANGLES):
        copies[a - 1].wait()
        images[a] = jnp.dot(half[...], tiles[a - 1], preferred_element_type=F32)


def project_near(angles, after, half, from_pair, from_cross, tile, tiles, planes, near):
    del after
    slab_rows = half.shape[0]
    above = pair_is_above()
    pair_row = pl.multiple_of(jnp.where(above, 2 * slab_rows, 0), 16)
    cross_row = pl.multiple_of(jnp.where(above, 0, 2 * slab_rows), 16)
    near[pl.ds(slab_rows, slab_rows), :] = half[...]
    near[pl.ds(pair_row, slab_rows), :] = from_pair[...]
    near[pl.ds(cross_row, slab_rows), :] = from_cross[...]
    for k, a in enumerate(angles):
        weights = tile[...] if a == 0 else tiles[a - 1]
        image = jnp.dot(near[...], weights, preferred_element_type=F32)
        for j in range(image.shape[1] // LANES):
            planes[k, j] = image[:, j * LANES : (j + 1) * LANES]


def combine(own, from_pair, from_cross, tile, tiles, images, grad_sums, residual_part, image_part,
            sums):
    slab_rows = own.shape[0]
    cells, columns = tile.shape
    zero = jnp.zeros((1, LANES), F32)

    def gathered(cut):
        return own[:, cut] + from_pair[:, cut].astype(F32) + from_cross[:, cut].astype(F32)

    counts = gathered(slice(ANGLES * columns, ANGLES * columns + LANES))
    image_norm = zero
    for a in range(ANGLES):
        rows = gathered(slice(a * columns, (a + 1) * columns))
        image = images[a]
        weighted = counts[:, a : a + 1] * image
        image_norm = image_norm + lane_sums(weighted * image)
        both = jnp.concatenate([*split(rows), *split(weighted)], axis=0)
        weights = tile if a == 0 else tiles.at[a - 1]
        for b in range(0, cells, CHUNK):
            cut = slice(b, b + CHUNK)
            part = lax.dot_general(
                both, weights[cut, :], (((1,), (1,)), ((), ())), preferred_element_type=F32
            )
            r = part[:slab_rows] + part[slab_rows : 2 * slab_rows]
            i = part[2 * slab_rows : 3 * slab_rows] + part[3 * slab_rows :]
            if a == 0:
                residual_part[:, cut] = r
                image_part[:, cut] = i
            else:
                residual_part[:, cut] += r
                image_part[:, cut] += i

    rr, ri, ii = zero, zero, zero
    for b in range(0, cells, CHUNK):
        r, i = residual_part[:, b : b + CHUNK], image_part[:, b : b + CHUNK]
        rr, ri, ii = rr + lane_sums(r * r), ri + lane_sums(r * i), ii + lane_sums(i * i)
    sums[...] = jnp.concatenate(
        [grad_sums[...], image_norm, rr, ri, ii, zero, zero, zero], axis=0
    )


def finish(offsets, sums, solution, direction, residual_part, image_part, *refs):
    finish_planes(
        offsets, sums, solution, direction, residual_part, image_part,
        [refs[g].at[k] for g, angles in enumerate(GROUPS) for k in range(len(angles))],
        *refs[len(GROUPS) :],
    )


def finish_planes(offsets, sums, solution, direction, residual_part, image_part, planes, residual,
           solution_hbm, residual_hbm, gradient_hbm, direction_hbm, updated, small, sem, small_sem):
    views, detector_rows, columns = residual.shape
    slab_rows = solution.shape[0]
    total = jnp.sum(sums[...], axis=1, keepdims=True)
    grad_norm, image_norm = total[0:1], total[1:2]
    step = grad_norm / image_norm
    new_norm = total[2:3] - 2.0 * step * total[3:4] + step * step * total[4:5]
    beta = new_norm / grad_norm

    def out_copy(v):
        return pltpu.make_async_copy(updated.at[v], residual_hbm.at[v], sem.at[v])

    small_copies = [
        pltpu.make_async_copy(small.at[k], target, small_sem.at[k])
        for k, target in enumerate((gradient_hbm, solution_hbm, direction_hbm))
    ]
    gradient = residual_part[...] - step * image_part[...]
    small[0] = gradient
    small_copies[0].start()
    small[1] = solution[...] + step * direction[...]
    small_copies[1].start()
    small[2] = gradient + beta * direction[...]
    small_copies[2].start()
    for v in range(views):
        first = first_plane(offsets, v, slab_rows)
        for j in range(columns // LANES):
            cut = slice(j * LANES, (j + 1) * LANES)
            updated[v, :, cut] = (
                residual[v, :, cut] - step * planes[v % ANGLES][j, pl.ds(first, detector_rows), :]
            )
        out_copy(v).start()
    for c in small_copies:
        c.wait()
    for v in range(views):
        out_copy(v).wait()


def exchanged_sum(x, masks):
    count = lax.axis_size("slab")
    terms = [lax.ppermute(x, "slab", [(i, i ^ m) for i in range(count)]) for m in masks]
    for term in terms:
        x = x + term
    return x


def local(solution, direction, gradient, residual, tiles, offsets):
    slab_rows, cells = solution.shape
    views, detector_rows, columns = residual.shape
    near = 3 * slab_rows
    blocks = columns // LANES
    count = lax.axis_size("slab")
    pair = [(i, i ^ 1) for i in range(count)]
    cross = [(i, i + 1) for i in range(1, count - 1, 2)]
    cross = cross + [(i, j) for j, i in cross]

    vmem = pl.BlockSpec(memory_space=pltpu.VMEM)
    smem = pl.BlockSpec(memory_space=pltpu.SMEM)
    hbm = pl.BlockSpec(memory_space=pltpu.HBM)
    sds = jax.ShapeDtypeStruct

    wide = ANGLES * columns + LANES
    tiles = pltpu.with_memory_space_constraint(tiles, pltpu.HBM)
    own, to_pair, to_cross, residual_here, tile, half = pl.pallas_call(
        sum_residuals,
        name="sum_residuals",
        in_specs=[hbm] * 4,
        out_specs=[vmem] * 6,
        out_shape=[
            sds((slab_rows, wide), F32),
            sds((slab_rows, wide), BF16),
            sds((slab_rows, wide), BF16),
            pltpu.VMEM(residual.shape, F32),
            pltpu.VMEM(tiles.shape[1:], BF16),
            sds((slab_rows, cells), BF16),
        ],
        scratch_shapes=[
            pltpu.VMEM((wide // LANES, near, LANES), F32),
            pltpu.SMEM(offsets.shape, jnp.int32),
            pltpu.VMEM((slab_rows, cells), F32),
            pltpu.SemaphoreType.DMA((views,)),
            pltpu.SemaphoreType.DMA,
            pltpu.SemaphoreType.DMA,
            pltpu.SemaphoreType.DMA,
        ],
        compiler_params=pltpu.CompilerParams(vmem_limit_bytes=8 * MIB),
        cost_estimate=pl.CostEstimate(
            flops=residual.size, bytes_accessed=4 * residual.size, transcendentals=0
        ),
    )(
        pltpu.with_memory_space_constraint(offsets, pltpu.HBM),
        pltpu.with_memory_space_constraint(residual, pltpu.HBM),
        tiles,
        pltpu.with_memory_space_constraint(direction, pltpu.HBM),
    )

    from_cross = lax.ppermute(to_cross, "slab", cross)
    from_pair = lax.ppermute(to_pair, "slab", pair)
    half_cross = lax.ppermute(half, "slab", cross)
    half_pair = lax.ppermute(half, "slab", pair)

    images, grad_sums, tiles_here = pl.pallas_call(
        project_own,
        name="project_own",
        in_specs=[vmem] * 3 + [hbm],
        out_specs=[vmem] * 3,
        out_shape=[
            sds((ANGLES, slab_rows, columns), F32),
            sds((1, LANES), F32),
            pltpu.VMEM((ANGLES - 1, *tiles.shape[1:]), BF16),
        ],
        scratch_shapes=[pltpu.SemaphoreType.DMA((ANGLES - 1,))],
        compiler_params=pltpu.CompilerParams(vmem_limit_bytes=8 * MIB),
        cost_estimate=pl.CostEstimate(
            flops=2 * near * cells * columns * ANGLES, bytes_accessed=16 * MIB, transcendentals=0
        ),
    )(half, gradient, tile, tiles)

    residual_part, image_part, sums = pl.pallas_call(
        combine,
        name="combine",
        in_specs=[vmem] * 7,
        out_specs=[vmem] * 3,
        out_shape=[
            sds((slab_rows, cells), F32),
            sds((slab_rows, cells), F32),
            sds((8, LANES), F32),
        ],
        compiler_params=pltpu.CompilerParams(vmem_limit_bytes=8 * MIB),
    )(own, from_pair, from_cross, tile, tiles_here, images, grad_sums)

    planes = []
    for masks, angles in zip(ROUNDS, GROUPS):
        planes.append(
            pl.pallas_call(
                functools.partial(project_near, angles),
                name="project_near",
                in_specs=[vmem] * 6,
                out_specs=vmem,
                out_shape=sds((len(angles), blocks, near, LANES), F32),
                scratch_shapes=[pltpu.VMEM((near, cells), BF16)],
                compiler_params=pltpu.CompilerParams(vmem_limit_bytes=6 * MIB),
                cost_estimate=pl.CostEstimate(
                    flops=2 * near * cells * columns * len(angles),
                    bytes_accessed=MIB,
                    transcendentals=0,
                ),
            )(sums, half, half_pair, half_cross, tile, tiles_here)
        )
        sums = exchanged_sum(sums, masks)

    return pl.pallas_call(
        finish,
        name="finish",
        in_specs=[smem] + [vmem] * 9,
        out_specs=[hbm] * 4,
        out_shape=[
            sds(solution.shape, F32),
            sds(residual.shape, F32),
            sds(solution.shape, F32),
            sds(solution.shape, F32),
        ],
        scratch_shapes=[
            pltpu.VMEM(residual.shape, F32),
            pltpu.VMEM((3, slab_rows, cells), F32),
            pltpu.SemaphoreType.DMA((views,)),
            pltpu.SemaphoreType.DMA((3,)),
        ],
        compiler_params=pltpu.CompilerParams(vmem_limit_bytes=12 * MIB),
    )(offsets, sums, solution, direction, residual_part, image_part, *planes, residual_here)


def solution(mesh):
    placed = (
        P(("scan", "slab"), None),
        P(("scan", "slab"), None),
        P(("scan", "slab"), None),
        P(("scan", "slab"), None, None),
        P(),
        P(("scan", "slab")),
    )
    return jax.shard_map(
        local,
        mesh=mesh,
        in_specs=placed,
        out_specs=(
            P(("scan", "slab"), None),
            P(("scan", "slab"), None, None),
            P(("scan", "slab"), None),
            P(("scan", "slab"), None),
        ),
        check_vma=False,
    )
```

```python
import functools

import jax
import jax.numpy as jnp
from jax import lax
from jax.experimental import pallas as pl
from jax.experimental.pallas import tpu as pltpu
from jax.sharding import PartitionSpec as P

ANGLES = 4
LANES = 128
CHUNK = 512
ROUNDS = ((1, 2, 3), (8, 16, 24), (4,))
GROUPS = ((0,), (1,), (2, 3))
F32 = jnp.float32
BF16 = jnp.bfloat16
MIB = 1 << 20


def first_plane(offsets, v, slab_rows):
    return offsets[v] - lax.axis_index("slab") * slab_rows + slab_rows


def pair_is_above():
    return lax.rem(lax.axis_index("slab"), 2) == 0


def split(x):
    high = x.astype(BF16)
    return high, (x - high.astype(F32)).astype(BF16)


def lane_sums(x):
    total = x[:, :LANES]
    for j in range(1, x.shape[1] // LANES):
        total = total + x[:, j * LANES : (j + 1) * LANES]
    return jnp.sum(total, axis=0, keepdims=True)


def sum_residuals(offsets_hbm, residual_hbm, tiles_hbm, direction_hbm, own, to_pair, to_cross,
                  residual, tile, half, rows, offsets, direction, sem, offsets_sem, tile_sem,
                  direction_sem):
    views, detector_rows, columns = residual.shape
    slab_rows = own.shape[0]
    near = 3 * slab_rows
    blocks = columns // LANES

    def copy(v):
        return pltpu.make_async_copy(residual_hbm.at[v], residual.at[v], sem.at[v])

    offsets_copy = pltpu.make_async_copy(offsets_hbm, offsets, offsets_sem)
    offsets_copy.start()
    for v in range(views):
        copy(v).start()
    direction_copy = pltpu.make_async_copy(direction_hbm, direction, direction_sem)
    direction_copy.start()
    tile_copy = pltpu.make_async_copy(tiles_hbm.at[0], tile, tile_sem)
    tile_copy.start()
    above = pair_is_above()
    pair_row = pl.multiple_of(jnp.where(above, 2 * slab_rows, 0), 16)
    cross_row = pl.multiple_of(jnp.where(above, 0, 2 * slab_rows), 16)

    rows[: ANGLES * blocks] = jnp.zeros((ANGLES * blocks, near, LANES), F32)
    plane = lax.broadcasted_iota(jnp.int32, (near, LANES), 0)
    lane = lax.broadcasted_iota(jnp.int32, (near, LANES), 1)
    counts = jnp.zeros((near, LANES), F32)
    offsets_copy.wait()
    for v in range(views):
        first = first_plane(offsets, v, slab_rows)
        seen = (plane >= first) & (plane < first + detector_rows) & (lane == v % ANGLES)
        counts = counts + seen.astype(F32)
    rows[ANGLES * blocks] = counts

    for v in range(views):
        first = first_plane(offsets, v, slab_rows)
        copy(v).wait()
        for j in range(blocks):
            rows[v % ANGLES * blocks + j, pl.ds(first, detector_rows), :] += residual[
                v, :, j * LANES : (j + 1) * LANES
            ]
    for k in range(ANGLES * blocks + 1):
        cut = slice(k * LANES, (k + 1) * LANES)
        to_pair[:, cut] = rows[k, pl.ds(pair_row, slab_rows), :].astype(BF16)
        to_cross[:, cut] = rows[k, pl.ds(cross_row, slab_rows), :].astype(BF16)
        own[:, cut] = rows[k, slab_rows : 2 * slab_rows, :]
    direction_copy.wait()
    half[...] = direction[...].astype(BF16)
    to_pair[:, to_cross.shape[1] :] = half[...]
    tile_copy.wait()


def project_own(half, gradient, tile, tiles_hbm, images, grad_sums, tiles, to_cross, sem):
    copies = [
        pltpu.make_async_copy(tiles_hbm.at[a], tiles.at[a - 1], sem.at[a - 1])
        for a in range(1, ANGLES)
    ]
    for c in copies:
        c.start()
    grad_sums[...] = lane_sums(gradient[...] * gradient[...])
    to_cross[...] = half[...]
    images[0] = jnp.dot(half[...], tile[...], preferred_element_type=F32)
    for a in range(1, ANGLES):
        copies[a - 1].wait()
        images[a] = jnp.dot(half[...], tiles[a - 1], preferred_element_type=F32)


def project_near(angles, after, half, from_pair, from_cross, tile, tiles, planes, near):
    del after
    slab_rows = half.shape[0]
    above = pair_is_above()
    pair_row = pl.multiple_of(jnp.where(above, 2 * slab_rows, 0), 16)
    cross_row = pl.multiple_of(jnp.where(above, 0, 2 * slab_rows), 16)
    near[pl.ds(slab_rows, slab_rows), :] = half[...]
    near[pl.ds(pair_row, slab_rows), :] = from_pair[:, from_pair.shape[1] - half.shape[1] :]
    near[pl.ds(cross_row, slab_rows), :] = from_cross[...]
    for k, a in enumerate(angles):
        weights = tile[...] if a == 0 else tiles[a - 1]
        image = jnp.dot(near[...], weights, preferred_element_type=F32)
        for j in range(image.shape[1] // LANES):
            planes[k, j] = image[:, j * LANES : (j + 1) * LANES]


def combine(own, from_pair, from_cross, tile, tiles, images, grad_sums, residual_part, image_part,
            sums, both):
    slab_rows = own.shape[0]
    cells, columns = tile.shape
    zero = jnp.zeros((1, LANES), F32)

    def gathered(cut):
        return own[:, cut] + from_pair[:, cut].astype(F32) + from_cross[:, cut].astype(F32)

    counts = gathered(slice(ANGLES * columns, ANGLES * columns + LANES))
    image_norm = zero
    for a in range(ANGLES):
        cut = slice(a * columns, (a + 1) * columns)
        weighted = counts[:, a : a + 1] * images[a]
        image_norm = image_norm + lane_sums(weighted * images[a])
        for k, part in enumerate((*split(gathered(cut)), *split(weighted))):
            both[k * slab_rows : (k + 1) * slab_rows, cut] = part
    both[4 * slab_rows :, :] = jnp.zeros_like(both[4 * slab_rows :, :])

    rr, ri, ii = zero, zero, zero
    for b in range(0, cells, CHUNK):
        cut = slice(b, b + CHUNK)
        weights = jnp.concatenate(
            [tile[cut, :], *(tiles[a, cut, :] for a in range(ANGLES - 1))], axis=1
        )
        part = lax.dot_general(
            both[...], weights, (((1,), (1,)), ((), ())), preferred_element_type=F32
        )
        r = part[:slab_rows] + part[slab_rows : 2 * slab_rows]
        i = part[2 * slab_rows : 3 * slab_rows] + part[3 * slab_rows : 4 * slab_rows]
        residual_part[:, cut] = r
        image_part[:, cut] = i
        rr, ri, ii = rr + lane_sums(r * r), ri + lane_sums(r * i), ii + lane_sums(i * i)
    sums[...] = jnp.concatenate(
        [grad_sums[...], image_norm, rr, ri, ii, zero, zero, zero], axis=0
    )


def finish(offsets, sums, solution, direction, residual_part, image_part, *refs):
    finish_planes(
        offsets, sums, solution, direction, residual_part, image_part,
        [refs[g].at[k] for g, angles in enumerate(GROUPS) for k in range(len(angles))],
        *refs[len(GROUPS) :],
    )


def finish_planes(offsets, sums, solution, direction, residual_part, image_part, planes, residual,
           solution_hbm, residual_hbm, gradient_hbm, direction_hbm, updated, small, sem, small_sem):
    views, detector_rows, columns = residual.shape
    slab_rows = solution.shape[0]
    total = jnp.sum(sums[...], axis=1, keepdims=True)
    grad_norm, image_norm = total[0:1], total[1:2]
    step = grad_norm / image_norm
    new_norm = total[2:3] - 2.0 * step * total[3:4] + step * step * total[4:5]
    beta = new_norm / grad_norm

    def out_copy(v):
        return pltpu.make_async_copy(updated.at[v], residual_hbm.at[v], sem.at[v])

    small_copies = [
        pltpu.make_async_copy(small.at[k], target, small_sem.at[k])
        for k, target in enumerate((gradient_hbm, solution_hbm, direction_hbm))
    ]
    gradient = residual_part[...] - step * image_part[...]
    small[0] = gradient
    small_copies[0].start()
    small[1] = solution[...] + step * direction[...]
    small_copies[1].start()
    small[2] = gradient + beta * direction[...]
    small_copies[2].start()
    for v in range(views):
        first = first_plane(offsets, v, slab_rows)
        for j in range(columns // LANES):
            cut = slice(j * LANES, (j + 1) * LANES)
            updated[v, :, cut] = (
                residual[v, :, cut] - step * planes[v % ANGLES][j, pl.ds(first, detector_rows), :]
            )
        out_copy(v).start()
    for c in small_copies:
        c.wait()
    for v in range(views):
        out_copy(v).wait()


def exchanged_sum(x, masks):
    count = lax.axis_size("slab")
    terms = [lax.ppermute(x, "slab", [(i, i ^ m) for i in range(count)]) for m in masks]
    for term in terms:
        x = x + term
    return x


def local(solution, direction, gradient, residual, tiles, offsets):
    slab_rows, cells = solution.shape
    views, detector_rows, columns = residual.shape
    near = 3 * slab_rows
    blocks = columns // LANES
    count = lax.axis_size("slab")
    pair = [(i, i ^ 1) for i in range(count)]
    cross = [(i, i + 1) for i in range(1, count - 1, 2)]
    cross = cross + [(i, j) for j, i in cross]

    vmem = pl.BlockSpec(memory_space=pltpu.VMEM)
    smem = pl.BlockSpec(memory_space=pltpu.SMEM)
    hbm = pl.BlockSpec(memory_space=pltpu.HBM)
    sds = jax.ShapeDtypeStruct

    wide = ANGLES * columns + LANES
    tiles = pltpu.with_memory_space_constraint(tiles, pltpu.HBM)
    own, to_pair, to_cross, residual_here, tile, half = pl.pallas_call(
        sum_residuals,
        name="sum_residuals",
        in_specs=[hbm] * 4,
        out_specs=[vmem] * 6,
        out_shape=[
            sds((slab_rows, wide), F32),
            sds((slab_rows, wide + cells), BF16),
            sds((slab_rows, wide), BF16),
            pltpu.VMEM(residual.shape, F32),
            pltpu.VMEM(tiles.shape[1:], BF16),
            sds((slab_rows, cells), BF16),
        ],
        scratch_shapes=[
            pltpu.VMEM((wide // LANES, near, LANES), F32),
            pltpu.SMEM(offsets.shape, jnp.int32),
            pltpu.VMEM((slab_rows, cells), F32),
            pltpu.SemaphoreType.DMA((views,)),
            pltpu.SemaphoreType.DMA,
            pltpu.SemaphoreType.DMA,
            pltpu.SemaphoreType.DMA,
        ],
        compiler_params=pltpu.CompilerParams(vmem_limit_bytes=8 * MIB),
        cost_estimate=pl.CostEstimate(
            flops=residual.size, bytes_accessed=4 * residual.size, transcendentals=0
        ),
    )(
        pltpu.with_memory_space_constraint(offsets, pltpu.HBM),
        pltpu.with_memory_space_constraint(residual, pltpu.HBM),
        tiles,
        pltpu.with_memory_space_constraint(direction, pltpu.HBM),
    )

    from_cross = lax.ppermute(to_cross, "slab", cross)
    from_pair = lax.ppermute(to_pair, "slab", pair)

    images, grad_sums, tiles_here, half_to_cross = pl.pallas_call(
        project_own,
        name="project_own",
        in_specs=[vmem] * 3 + [hbm],
        out_specs=[vmem] * 4,
        out_shape=[
            sds((ANGLES, slab_rows, columns), F32),
            sds((1, LANES), F32),
            pltpu.VMEM((ANGLES - 1, *tiles.shape[1:]), BF16),
            sds((slab_rows, cells), BF16),
        ],
        scratch_shapes=[pltpu.SemaphoreType.DMA((ANGLES - 1,))],
        compiler_params=pltpu.CompilerParams(vmem_limit_bytes=8 * MIB),
        cost_estimate=pl.CostEstimate(
            flops=2 * near * cells * columns * ANGLES, bytes_accessed=16 * MIB, transcendentals=0
        ),
    )(half, gradient, tile, tiles)

    half_cross = lax.ppermute(half_to_cross, "slab", cross)

    residual_part, image_part, sums = pl.pallas_call(
        combine,
        name="combine",
        in_specs=[vmem] * 7,
        out_specs=[vmem] * 3,
        out_shape=[
            sds((slab_rows, cells), F32),
            sds((slab_rows, cells), F32),
            sds((8, LANES), F32),
        ],
        scratch_shapes=[pltpu.VMEM((256, ANGLES * columns), BF16)],
        compiler_params=pltpu.CompilerParams(vmem_limit_bytes=8 * MIB),
    )(own, from_pair, from_cross, tile, tiles_here, images, grad_sums)

    planes = []
    for masks, angles in zip(ROUNDS, GROUPS):
        planes.append(
            pl.pallas_call(
                functools.partial(project_near, angles),
                name="project_near",
                in_specs=[vmem] * 6,
                out_specs=vmem,
                out_shape=sds((len(angles), blocks, near, LANES), F32),
                scratch_shapes=[pltpu.VMEM((near, cells), BF16)],
                compiler_params=pltpu.CompilerParams(vmem_limit_bytes=6 * MIB),
                cost_estimate=pl.CostEstimate(
                    flops=2 * near * cells * columns * len(angles),
                    bytes_accessed=MIB,
                    transcendentals=0,
                ),
            )(sums, half, from_pair, half_cross, tile, tiles_here)
        )
        sums = exchanged_sum(sums, masks)

    return pl.pallas_call(
        finish,
        name="finish",
        in_specs=[smem] + [vmem] * 9,
        out_specs=[hbm] * 4,
        out_shape=[
            sds(solution.shape, F32),
            sds(residual.shape, F32),
            sds(solution.shape, F32),
            sds(solution.shape, F32),
        ],
        scratch_shapes=[
            pltpu.VMEM(residual.shape, F32),
            pltpu.VMEM((3, slab_rows, cells), F32),
            pltpu.SemaphoreType.DMA((views,)),
            pltpu.SemaphoreType.DMA((3,)),
        ],
        compiler_params=pltpu.CompilerParams(vmem_limit_bytes=12 * MIB),
    )(offsets, sums, solution, direction, residual_part, image_part, *planes, residual_here)


def solution(mesh):
    placed = (
        P(("scan", "slab"), None),
        P(("scan", "slab"), None),
        P(("scan", "slab"), None),
        P(("scan", "slab"), None, None),
        P(),
        P(("scan", "slab")),
    )
    return jax.shard_map(
        local,
        mesh=mesh,
        in_specs=placed,
        out_specs=(
            P(("scan", "slab"), None),
            P(("scan", "slab"), None, None),
            P(("scan", "slab"), None),
            P(("scan", "slab"), None),
        ),
        check_vma=False,
    )
```

```python
import functools

import jax
import jax.numpy as jnp
from jax import lax
from jax.experimental import pallas as pl
from jax.experimental.pallas import tpu as pltpu
from jax.sharding import PartitionSpec as P

ANGLES = 4
LANES = 128
CHUNK = 512
ROUNDS = ((1, 2, 3), (8, 24, 16), (6,))
GROUPS = ((0,), (1,), (2, 3))
F32 = jnp.float32
BF16 = jnp.bfloat16
MIB = 1 << 20


def first_plane(offsets, v, slab_rows):
    return offsets[v] - lax.axis_index("slab") * slab_rows + slab_rows


def pair_is_above():
    return lax.rem(lax.axis_index("slab"), 2) == 0


def split(x):
    high = x.astype(BF16)
    return high, (x - high.astype(F32)).astype(BF16)


def lane_sums(x):
    total = x[:, :LANES]
    for j in range(1, x.shape[1] // LANES):
        total = total + x[:, j * LANES : (j + 1) * LANES]
    return jnp.sum(total, axis=0, keepdims=True)


def sum_residuals(offsets_hbm, residual_hbm, tiles_hbm, direction_hbm, own, to_pair, to_cross,
                  residual, tile, half, rows, offsets, direction, sem, offsets_sem, tile_sem,
                  direction_sem):
    views, detector_rows, columns = residual.shape
    slab_rows = own.shape[0]
    near = 3 * slab_rows
    blocks = columns // LANES

    def copy(v):
        return pltpu.make_async_copy(residual_hbm.at[v], residual.at[v], sem.at[v])

    offsets_copy = pltpu.make_async_copy(offsets_hbm, offsets, offsets_sem)
    offsets_copy.start()
    for v in range(views):
        copy(v).start()
    direction_copy = pltpu.make_async_copy(direction_hbm, direction, direction_sem)
    direction_copy.start()
    tile_copy = pltpu.make_async_copy(tiles_hbm.at[0], tile, tile_sem)
    tile_copy.start()
    above = pair_is_above()
    pair_row = pl.multiple_of(jnp.where(above, 2 * slab_rows, 0), 16)
    cross_row = pl.multiple_of(jnp.where(above, 0, 2 * slab_rows), 16)

    rows[: ANGLES * blocks] = jnp.zeros((ANGLES * blocks, near, LANES), F32)
    plane = lax.broadcasted_iota(jnp.int32, (near, LANES), 0)
    lane = lax.broadcasted_iota(jnp.int32, (near, LANES), 1)
    counts = jnp.zeros((near, LANES), F32)
    offsets_copy.wait()
    for v in range(views):
        first = first_plane(offsets, v, slab_rows)
        seen = (plane >= first) & (plane < first + detector_rows) & (lane == v % ANGLES)
        counts = counts + seen.astype(F32)
    rows[ANGLES * blocks] = counts

    for v in range(views):
        first = first_plane(offsets, v, slab_rows)
        copy(v).wait()
        for j in range(blocks):
            rows[v % ANGLES * blocks + j, pl.ds(first, detector_rows), :] += residual[
                v, :, j * LANES : (j + 1) * LANES
            ]
    for k in range(ANGLES * blocks + 1):
        cut = slice(k * LANES, (k + 1) * LANES)
        to_pair[:, cut] = rows[k, pl.ds(pair_row, slab_rows), :].astype(BF16)
        to_cross[:, cut] = rows[k, pl.ds(cross_row, slab_rows), :].astype(BF16)
        own[:, cut] = rows[k, slab_rows : 2 * slab_rows, :]
    direction_copy.wait()
    half[...] = direction[...].astype(BF16)
    to_pair[:, to_cross.shape[1] :] = half[...]
    tile_copy.wait()


def project_own(half, gradient, tile, tiles_hbm, images, grad_sums, tiles, to_cross, sem):
    copies = [
        pltpu.make_async_copy(tiles_hbm.at[a], tiles.at[a - 1], sem.at[a - 1])
        for a in range(1, ANGLES)
    ]
    for c in copies:
        c.start()
    grad_sums[...] = lane_sums(gradient[...] * gradient[...])
    to_cross[...] = half[...]
    images[0] = jnp.dot(half[...], tile[...], preferred_element_type=F32)
    for a in range(1, ANGLES):
        copies[a - 1].wait()
        images[a] = jnp.dot(half[...], tiles[a - 1], preferred_element_type=F32)


def project_near(angles, after, half, from_pair, from_cross, tile, tiles, planes, near):
    del after
    slab_rows = half.shape[0]
    above = pair_is_above()
    pair_row = pl.multiple_of(jnp.where(above, 2 * slab_rows, 0), 16)
    cross_row = pl.multiple_of(jnp.where(above, 0, 2 * slab_rows), 16)
    near[pl.ds(slab_rows, slab_rows), :] = half[...]
    near[pl.ds(pair_row, slab_rows), :] = from_pair[:, from_pair.shape[1] - half.shape[1] :]
    near[pl.ds(cross_row, slab_rows), :] = from_cross[...]
    for k, a in enumerate(angles):
        weights = tile[...] if a == 0 else tiles[a - 1]
        image = jnp.dot(near[...], weights, preferred_element_type=F32)
        for j in range(image.shape[1] // LANES):
            planes[k, j] = image[:, j * LANES : (j + 1) * LANES]


def combine(own, from_pair, from_cross, tile, tiles, images, grad_sums, residual_part, image_part,
            sums, both):
    slab_rows = own.shape[0]
    cells, columns = tile.shape
    zero = jnp.zeros((1, LANES), F32)

    def gathered(cut):
        return own[:, cut] + from_pair[:, cut].astype(F32) + from_cross[:, cut].astype(F32)

    counts = gathered(slice(ANGLES * columns, ANGLES * columns + LANES))
    image_norm = zero
    for a in range(ANGLES):
        cut = slice(a * columns, (a + 1) * columns)
        weighted = counts[:, a : a + 1] * images[a]
        image_norm = image_norm + lane_sums(weighted * images[a])
        for k, part in enumerate((*split(gathered(cut)), *split(weighted))):
            both[k * slab_rows : (k + 1) * slab_rows, cut] = part
    both[4 * slab_rows :, :] = jnp.zeros_like(both[4 * slab_rows :, :])

    rr, ri, ii = zero, zero, zero
    for b in range(0, cells, CHUNK):
        cut = slice(b, b + CHUNK)
        weights = jnp.concatenate(
            [tile[cut, :], *(tiles[a, cut, :] for a in range(ANGLES - 1))], axis=1
        )
        part = lax.dot_general(
            both[...], weights, (((1,), (1,)), ((), ())), preferred_element_type=F32
        )
        r = part[:slab_rows] + part[slab_rows : 2 * slab_rows]
        i = part[2 * slab_rows : 3 * slab_rows] + part[3 * slab_rows : 4 * slab_rows]
        residual_part[:, cut] = r
        image_part[:, cut] = i
        rr, ri, ii = rr + lane_sums(r * r), ri + lane_sums(r * i), ii + lane_sums(i * i)
    sums[...] = jnp.concatenate(
        [grad_sums[...], image_norm, rr, ri, ii, zero, zero, zero], axis=0
    )


def finish(offsets, sums, solution, direction, residual_part, image_part, *refs):
    finish_planes(
        offsets, sums, solution, direction, residual_part, image_part,
        [refs[g].at[k] for g, angles in enumerate(GROUPS) for k in range(len(angles))],
        *refs[len(GROUPS) :],
    )


def finish_planes(offsets, sums, solution, direction, residual_part, image_part, planes, residual,
           solution_hbm, residual_hbm, gradient_hbm, direction_hbm, updated, small, sem, small_sem):
    views, detector_rows, columns = residual.shape
    slab_rows = solution.shape[0]
    total = jnp.sum(sums[...], axis=1, keepdims=True)
    grad_norm, image_norm = total[0:1], total[1:2]
    step = grad_norm / image_norm
    new_norm = total[2:3] - 2.0 * step * total[3:4] + step * step * total[4:5]
    beta = new_norm / grad_norm

    def out_copy(v):
        return pltpu.make_async_copy(updated.at[v], residual_hbm.at[v], sem.at[v])

    small_copies = [
        pltpu.make_async_copy(small.at[k], target, small_sem.at[k])
        for k, target in enumerate((gradient_hbm, solution_hbm, direction_hbm))
    ]
    gradient = residual_part[...] - step * image_part[...]
    small[0] = gradient
    small_copies[0].start()
    small[1] = solution[...] + step * direction[...]
    small_copies[1].start()
    small[2] = gradient + beta * direction[...]
    small_copies[2].start()
    for v in range(views):
        first = first_plane(offsets, v, slab_rows)
        for j in range(columns // LANES):
            cut = slice(j * LANES, (j + 1) * LANES)
            updated[v, :, cut] = (
                residual[v, :, cut] - step * planes[v % ANGLES][j, pl.ds(first, detector_rows), :]
            )
        out_copy(v).start()
    for c in small_copies:
        c.wait()
    for v in range(views):
        out_copy(v).wait()


def exchanged_sum(x, masks):
    count = lax.axis_size("slab")
    terms = [lax.ppermute(x, "slab", [(i, i ^ m) for i in range(count)]) for m in masks]
    for term in terms:
        x = x + term
    return x


def local(solution, direction, gradient, residual, tiles, offsets):
    slab_rows, cells = solution.shape
    views, detector_rows, columns = residual.shape
    near = 3 * slab_rows
    blocks = columns // LANES
    count = lax.axis_size("slab")
    pair = [(i, i ^ 1) for i in range(count)]
    cross = [(i, i + 1) for i in range(1, count - 1, 2)]
    cross = cross + [(i, j) for j, i in cross]

    vmem = pl.BlockSpec(memory_space=pltpu.VMEM)
    smem = pl.BlockSpec(memory_space=pltpu.SMEM)
    hbm = pl.BlockSpec(memory_space=pltpu.HBM)
    sds = jax.ShapeDtypeStruct

    wide = ANGLES * columns + LANES
    tiles = pltpu.with_memory_space_constraint(tiles, pltpu.HBM)
    own, to_pair, to_cross, residual_here, tile, half = pl.pallas_call(
        sum_residuals,
        name="sum_residuals",
        in_specs=[hbm] * 4,
        out_specs=[vmem] * 6,
        out_shape=[
            sds((slab_rows, wide), F32),
            sds((slab_rows, wide + cells), BF16),
            sds((slab_rows, wide), BF16),
            pltpu.VMEM(residual.shape, F32),
            pltpu.VMEM(tiles.shape[1:], BF16),
            sds((slab_rows, cells), BF16),
        ],
        scratch_shapes=[
            pltpu.VMEM((wide // LANES, near, LANES), F32),
            pltpu.SMEM(offsets.shape, jnp.int32),
            pltpu.VMEM((slab_rows, cells), F32),
            pltpu.SemaphoreType.DMA((views,)),
            pltpu.SemaphoreType.DMA,
            pltpu.SemaphoreType.DMA,
            pltpu.SemaphoreType.DMA,
        ],
        compiler_params=pltpu.CompilerParams(vmem_limit_bytes=8 * MIB),
        cost_estimate=pl.CostEstimate(
            flops=residual.size, bytes_accessed=4 * residual.size, transcendentals=0
        ),
    )(
        pltpu.with_memory_space_constraint(offsets, pltpu.HBM),
        pltpu.with_memory_space_constraint(residual, pltpu.HBM),
        tiles,
        pltpu.with_memory_space_constraint(direction, pltpu.HBM),
    )

    from_cross = lax.ppermute(to_cross, "slab", cross)
    from_pair = lax.ppermute(to_pair, "slab", pair)

    images, grad_sums, tiles_here, half_to_cross = pl.pallas_call(
        project_own,
        name="project_own",
        in_specs=[vmem] * 3 + [hbm],
        out_specs=[vmem] * 4,
        out_shape=[
            sds((ANGLES, slab_rows, columns), F32),
            sds((1, LANES), F32),
            pltpu.VMEM((ANGLES - 1, *tiles.shape[1:]), BF16),
            sds((slab_rows, cells), BF16),
        ],
        scratch_shapes=[pltpu.SemaphoreType.DMA((ANGLES - 1,))],
        compiler_params=pltpu.CompilerParams(vmem_limit_bytes=8 * MIB),
        cost_estimate=pl.CostEstimate(
            flops=2 * near * cells * columns * ANGLES, bytes_accessed=16 * MIB, transcendentals=0
        ),
    )(half, gradient, tile, tiles)

    half_cross = lax.ppermute(half_to_cross, "slab", cross)

    residual_part, image_part, sums = pl.pallas_call(
        combine,
        name="combine",
        in_specs=[vmem] * 7,
        out_specs=[vmem] * 3,
        out_shape=[
            sds((slab_rows, cells), F32),
            sds((slab_rows, cells), F32),
            sds((8, LANES), F32),
        ],
        scratch_shapes=[pltpu.VMEM((256, ANGLES * columns), BF16)],
        compiler_params=pltpu.CompilerParams(vmem_limit_bytes=8 * MIB),
    )(own, from_pair, from_cross, tile, tiles_here, images, grad_sums)

    planes = []
    for masks, angles in zip(ROUNDS, GROUPS):
        planes.append(
            pl.pallas_call(
                functools.partial(project_near, angles),
                name="project_near",
                in_specs=[vmem] * 6,
                out_specs=vmem,
                out_shape=sds((len(angles), blocks, near, LANES), F32),
                scratch_shapes=[pltpu.VMEM((near, cells), BF16)],
                compiler_params=pltpu.CompilerParams(vmem_limit_bytes=6 * MIB),
                cost_estimate=pl.CostEstimate(
                    flops=2 * near * cells * columns * len(angles),
                    bytes_accessed=MIB,
                    transcendentals=0,
                ),
            )(sums, half, from_pair, half_cross, tile, tiles_here)
        )
        sums = exchanged_sum(sums, masks)

    return pl.pallas_call(
        finish,
        name="finish",
        in_specs=[smem] + [vmem] * 9,
        out_specs=[hbm] * 4,
        out_shape=[
            sds(solution.shape, F32),
            sds(residual.shape, F32),
            sds(solution.shape, F32),
            sds(solution.shape, F32),
        ],
        scratch_shapes=[
            pltpu.VMEM(residual.shape, F32),
            pltpu.VMEM((3, slab_rows, cells), F32),
            pltpu.SemaphoreType.DMA((views,)),
            pltpu.SemaphoreType.DMA((3,)),
        ],
        compiler_params=pltpu.CompilerParams(vmem_limit_bytes=12 * MIB),
    )(offsets, sums, solution, direction, residual_part, image_part, *planes, residual_here)


def solution(mesh):
    placed = (
        P(("scan", "slab"), None),
        P(("scan", "slab"), None),
        P(("scan", "slab"), None),
        P(("scan", "slab"), None, None),
        P(),
        P(("scan", "slab")),
    )
    return jax.shard_map(
        local,
        mesh=mesh,
        in_specs=placed,
        out_specs=(
            P(("scan", "slab"), None),
            P(("scan", "slab"), None, None),
            P(("scan", "slab"), None),
            P(("scan", "slab"), None),
        ),
        check_vma=False,
    )
```

```python
import functools

import jax
import jax.numpy as jnp
from jax import lax
from jax.experimental import pallas as pl
from jax.experimental.pallas import tpu as pltpu
from jax.sharding import PartitionSpec as P

ANGLES = 4
LANES = 128
CHUNK = 512
ROUNDS = ((1, 2, 3), (8, 24, 16), (6,))
GROUPS = ((0,), (1,), (2, 3))
F32 = jnp.float32
BF16 = jnp.bfloat16
MIB = 1 << 20


def first_plane(offsets, v, slab_rows):
    return offsets[v] - lax.axis_index("slab") * slab_rows + slab_rows


def pair_is_above():
    return lax.rem(lax.axis_index("slab"), 2) == 0


def split(x):
    high = x.astype(BF16)
    return high, (x - high.astype(F32)).astype(BF16)


def lane_sums(x):
    total = x[:, :LANES]
    for j in range(1, x.shape[1] // LANES):
        total = total + x[:, j * LANES : (j + 1) * LANES]
    return jnp.sum(total, axis=0, keepdims=True)


def sum_residuals(offsets_hbm, residual_hbm, direction_hbm, own, to_pair, to_cross, residual, half,
                  rows, offsets, direction, sem, offsets_sem, direction_sem):
    views, detector_rows, columns = residual.shape
    slab_rows = own.shape[0]
    near = 3 * slab_rows
    blocks = columns // LANES

    def copy(v):
        return pltpu.make_async_copy(residual_hbm.at[v], residual.at[v], sem.at[v])

    offsets_copy = pltpu.make_async_copy(offsets_hbm, offsets, offsets_sem)
    offsets_copy.start()
    for v in range(views):
        copy(v).start()
    direction_copy = pltpu.make_async_copy(direction_hbm, direction, direction_sem)
    direction_copy.start()
    above = pair_is_above()
    pair_row = pl.multiple_of(jnp.where(above, 2 * slab_rows, 0), 16)
    cross_row = pl.multiple_of(jnp.where(above, 0, 2 * slab_rows), 16)

    rows[: ANGLES * blocks] = jnp.zeros((ANGLES * blocks, near, LANES), F32)
    plane = lax.broadcasted_iota(jnp.int32, (near, LANES), 0)
    lane = lax.broadcasted_iota(jnp.int32, (near, LANES), 1)
    counts = jnp.zeros((near, LANES), F32)
    offsets_copy.wait()
    for v in range(views):
        first = first_plane(offsets, v, slab_rows)
        seen = (plane >= first) & (plane < first + detector_rows) & (lane == v % ANGLES)
        counts = counts + seen.astype(F32)
    rows[ANGLES * blocks] = counts

    for v in range(views):
        first = first_plane(offsets, v, slab_rows)
        copy(v).wait()
        for j in range(blocks):
            rows[v % ANGLES * blocks + j, pl.ds(first, detector_rows), :] += residual[
                v, :, j * LANES : (j + 1) * LANES
            ]
    for k in range(ANGLES * blocks + 1):
        cut = slice(k * LANES, (k + 1) * LANES)
        to_pair[:, cut] = rows[k, pl.ds(pair_row, slab_rows), :].astype(BF16)
        to_cross[:, cut] = rows[k, pl.ds(cross_row, slab_rows), :].astype(BF16)
        own[:, cut] = rows[k, slab_rows : 2 * slab_rows, :]
    direction_copy.wait()
    half[...] = direction[...].astype(BF16)
    to_pair[:, to_cross.shape[1] :] = half[...]


def project_own(half, gradient, tiles_hbm, images, grad_sums, tile, tiles, to_cross, sem):
    copies = [
        pltpu.make_async_copy(tiles_hbm.at[a], tile if a == 0 else tiles.at[a - 1], sem.at[a])
        for a in range(ANGLES)
    ]
    for c in copies:
        c.start()
    grad_sums[...] = lane_sums(gradient[...] * gradient[...])
    to_cross[...] = half[...]
    for a in range(ANGLES):
        copies[a].wait()
        weights = tile[...] if a == 0 else tiles[a - 1]
        images[a] = jnp.dot(half[...], weights, preferred_element_type=F32)


def project_near(angles, after, half, from_pair, from_cross, tile, tiles, planes, near):
    del after
    slab_rows = half.shape[0]
    above = pair_is_above()
    pair_row = pl.multiple_of(jnp.where(above, 2 * slab_rows, 0), 16)
    cross_row = pl.multiple_of(jnp.where(above, 0, 2 * slab_rows), 16)
    near[pl.ds(slab_rows, slab_rows), :] = half[...]
    near[pl.ds(pair_row, slab_rows), :] = from_pair[:, from_pair.shape[1] - half.shape[1] :]
    near[pl.ds(cross_row, slab_rows), :] = from_cross[...]
    for k, a in enumerate(angles):
        weights = tile[...] if a == 0 else tiles[a - 1]
        image = jnp.dot(near[...], weights, preferred_element_type=F32)
        for j in range(image.shape[1] // LANES):
            planes[k, j] = image[:, j * LANES : (j + 1) * LANES]


def combine(own, from_pair, from_cross, tile, tiles, images, grad_sums, residual_part, image_part,
            sums, both):
    slab_rows = own.shape[0]
    cells, columns = tile.shape
    zero = jnp.zeros((1, LANES), F32)

    def gathered(cut):
        return own[:, cut] + from_pair[:, cut].astype(F32) + from_cross[:, cut].astype(F32)

    counts = gathered(slice(ANGLES * columns, ANGLES * columns + LANES))
    image_norm = zero
    for a in range(ANGLES):
        cut = slice(a * columns, (a + 1) * columns)
        weighted = counts[:, a : a + 1] * images[a]
        image_norm = image_norm + lane_sums(weighted * images[a])
        for k, part in enumerate((*split(gathered(cut)), *split(weighted))):
            both[k * slab_rows : (k + 1) * slab_rows, cut] = part
    both[4 * slab_rows :, :] = jnp.zeros_like(both[4 * slab_rows :, :])

    rr, ri, ii = zero, zero, zero
    for b in range(0, cells, CHUNK):
        cut = slice(b, b + CHUNK)
        weights = jnp.concatenate(
            [tile[cut, :], *(tiles[a, cut, :] for a in range(ANGLES - 1))], axis=1
        )
        part = lax.dot_general(
            both[...], weights, (((1,), (1,)), ((), ())), preferred_element_type=F32
        )
        r = part[:slab_rows] + part[slab_rows : 2 * slab_rows]
        i = part[2 * slab_rows : 3 * slab_rows] + part[3 * slab_rows : 4 * slab_rows]
        residual_part[:, cut] = r
        image_part[:, cut] = i
        rr, ri, ii = rr + lane_sums(r * r), ri + lane_sums(r * i), ii + lane_sums(i * i)
    sums[...] = jnp.concatenate(
        [grad_sums[...], image_norm, rr, ri, ii, zero, zero, zero], axis=0
    )


def finish(offsets, sums, solution, direction, residual_part, image_part, *refs):
    finish_planes(
        offsets, sums, solution, direction, residual_part, image_part,
        [refs[g].at[k] for g, angles in enumerate(GROUPS) for k in range(len(angles))],
        *refs[len(GROUPS) :],
    )


def finish_planes(offsets, sums, solution, direction, residual_part, image_part, planes, residual,
           solution_hbm, residual_hbm, gradient_hbm, direction_hbm, updated, small, sem, small_sem):
    views, detector_rows, columns = residual.shape
    slab_rows = solution.shape[0]
    total = jnp.sum(sums[...], axis=1, keepdims=True)
    grad_norm, image_norm = total[0:1], total[1:2]
    step = grad_norm / image_norm
    new_norm = total[2:3] - 2.0 * step * total[3:4] + step * step * total[4:5]
    beta = new_norm / grad_norm

    def out_copy(v):
        return pltpu.make_async_copy(updated.at[v], residual_hbm.at[v], sem.at[v])

    small_copies = [
        pltpu.make_async_copy(small.at[k], target, small_sem.at[k])
        for k, target in enumerate((gradient_hbm, solution_hbm, direction_hbm))
    ]
    gradient = residual_part[...] - step * image_part[...]
    small[0] = gradient
    small_copies[0].start()
    small[1] = solution[...] + step * direction[...]
    small_copies[1].start()
    small[2] = gradient + beta * direction[...]
    small_copies[2].start()
    for v in range(views):
        first = first_plane(offsets, v, slab_rows)
        for j in range(columns // LANES):
            cut = slice(j * LANES, (j + 1) * LANES)
            updated[v, :, cut] = (
                residual[v, :, cut] - step * planes[v % ANGLES][j, pl.ds(first, detector_rows), :]
            )
        out_copy(v).start()
    for c in small_copies:
        c.wait()
    for v in range(views):
        out_copy(v).wait()


def exchanged_sum(x, masks):
    count = lax.axis_size("slab")
    terms = [lax.ppermute(x, "slab", [(i, i ^ m) for i in range(count)]) for m in masks]
    for term in terms:
        x = x + term
    return x


def local(solution, direction, gradient, residual, tiles, offsets):
    slab_rows, cells = solution.shape
    views, detector_rows, columns = residual.shape
    near = 3 * slab_rows
    blocks = columns // LANES
    count = lax.axis_size("slab")
    pair = [(i, i ^ 1) for i in range(count)]
    cross = [(i, i + 1) for i in range(1, count - 1, 2)]
    cross = cross + [(i, j) for j, i in cross]

    vmem = pl.BlockSpec(memory_space=pltpu.VMEM)
    smem = pl.BlockSpec(memory_space=pltpu.SMEM)
    hbm = pl.BlockSpec(memory_space=pltpu.HBM)
    sds = jax.ShapeDtypeStruct

    wide = ANGLES * columns + LANES
    tiles = pltpu.with_memory_space_constraint(tiles, pltpu.HBM)
    own, to_pair, to_cross, residual_here, half = pl.pallas_call(
        sum_residuals,
        name="sum_residuals",
        in_specs=[hbm] * 3,
        out_specs=[vmem] * 5,
        out_shape=[
            sds((slab_rows, wide), F32),
            sds((slab_rows, wide + cells), BF16),
            sds((slab_rows, wide), BF16),
            pltpu.VMEM(residual.shape, F32),
            sds((slab_rows, cells), BF16),
        ],
        scratch_shapes=[
            pltpu.VMEM((wide // LANES, near, LANES), F32),
            pltpu.SMEM(offsets.shape, jnp.int32),
            pltpu.VMEM((slab_rows, cells), F32),
            pltpu.SemaphoreType.DMA((views,)),
            pltpu.SemaphoreType.DMA,
            pltpu.SemaphoreType.DMA,
        ],
        compiler_params=pltpu.CompilerParams(vmem_limit_bytes=8 * MIB),
        cost_estimate=pl.CostEstimate(
            flops=residual.size, bytes_accessed=4 * residual.size, transcendentals=0
        ),
    )(
        pltpu.with_memory_space_constraint(offsets, pltpu.HBM),
        pltpu.with_memory_space_constraint(residual, pltpu.HBM),
        pltpu.with_memory_space_constraint(direction, pltpu.HBM),
    )

    from_cross = lax.ppermute(to_cross, "slab", cross)
    from_pair = lax.ppermute(to_pair, "slab", pair)

    images, grad_sums, tile, tiles_here, half_to_cross = pl.pallas_call(
        project_own,
        name="project_own",
        in_specs=[vmem] * 2 + [hbm],
        out_specs=[vmem] * 5,
        out_shape=[
            sds((ANGLES, slab_rows, columns), F32),
            sds((1, LANES), F32),
            pltpu.VMEM(tiles.shape[1:], BF16),
            pltpu.VMEM((ANGLES - 1, *tiles.shape[1:]), BF16),
            sds((slab_rows, cells), BF16),
        ],
        scratch_shapes=[pltpu.SemaphoreType.DMA((ANGLES,))],
        compiler_params=pltpu.CompilerParams(vmem_limit_bytes=8 * MIB),
        cost_estimate=pl.CostEstimate(
            flops=2 * near * cells * columns * ANGLES, bytes_accessed=16 * MIB, transcendentals=0
        ),
    )(half, gradient, tiles)

    half_cross = lax.ppermute(half_to_cross, "slab", cross)

    residual_part, image_part, sums = pl.pallas_call(
        combine,
        name="combine",
        in_specs=[vmem] * 7,
        out_specs=[vmem] * 3,
        out_shape=[
            sds((slab_rows, cells), F32),
            sds((slab_rows, cells), F32),
            sds((8, LANES), F32),
        ],
        scratch_shapes=[pltpu.VMEM((256, ANGLES * columns), BF16)],
        compiler_params=pltpu.CompilerParams(vmem_limit_bytes=8 * MIB),
    )(own, from_pair, from_cross, tile, tiles_here, images, grad_sums)

    planes = []
    for masks, angles in zip(ROUNDS, GROUPS):
        planes.append(
            pl.pallas_call(
                functools.partial(project_near, angles),
                name="project_near",
                in_specs=[vmem] * 6,
                out_specs=vmem,
                out_shape=sds((len(angles), blocks, near, LANES), F32),
                scratch_shapes=[pltpu.VMEM((near, cells), BF16)],
                compiler_params=pltpu.CompilerParams(vmem_limit_bytes=6 * MIB),
                cost_estimate=pl.CostEstimate(
                    flops=2 * near * cells * columns * len(angles),
                    bytes_accessed=MIB,
                    transcendentals=0,
                ),
            )(sums, half, from_pair, half_cross, tile, tiles_here)
        )
        sums = exchanged_sum(sums, masks)

    return pl.pallas_call(
        finish,
        name="finish",
        in_specs=[smem] + [vmem] * 9,
        out_specs=[hbm] * 4,
        out_shape=[
            sds(solution.shape, F32),
            sds(residual.shape, F32),
            sds(solution.shape, F32),
            sds(solution.shape, F32),
        ],
        scratch_shapes=[
            pltpu.VMEM(residual.shape, F32),
            pltpu.VMEM((3, slab_rows, cells), F32),
            pltpu.SemaphoreType.DMA((views,)),
            pltpu.SemaphoreType.DMA((3,)),
        ],
        compiler_params=pltpu.CompilerParams(vmem_limit_bytes=12 * MIB),
    )(offsets, sums, solution, direction, residual_part, image_part, *planes, residual_here)


def solution(mesh):
    placed = (
        P(("scan", "slab"), None),
        P(("scan", "slab"), None),
        P(("scan", "slab"), None),
        P(("scan", "slab"), None, None),
        P(),
        P(("scan", "slab")),
    )
    return jax.shard_map(
        local,
        mesh=mesh,
        in_specs=placed,
        out_specs=(
            P(("scan", "slab"), None),
            P(("scan", "slab"), None, None),
            P(("scan", "slab"), None),
            P(("scan", "slab"), None),
        ),
        check_vma=False,
    )
```
